256 devices in a mesh: region: 16 (over z, core), layer: 16 (over x, y).
Axes of the slice: x: 4, y: 4, z: 8, core: 2. Of those that a mesh axis runs over, the one named last changes fastest.
Arguments:
- right_side: float32 [64, 1048576], P(None, ('region', 'layer')), may hold values from -72 to 72
- block_entries: float32 [16384, 7, 4096], P(('region', 'layer')), may hold values from -0.01875 to 2.01875, as said below
- neighbours: int32 [16384, 6], P(('region', 'layer')), may hold values from 0 to 95
- face_rows: int32 [1024, 8], P(('region', 'layer')), may hold values from 0 to 63
- die_owner: int32 [131072, 1], P(('region', 'layer')), may hold values from 0 to 15; in each aligned block of 512 rows (0 to 511, 512 to 1023, ...) at most 128 rows name the same one
- die_node: int32 [131072], P(('region', 'layer')), may hold values from 0 to 4095
Outputs:
- solution_field: float32 [64, 1048576], P(None, ('region', 'layer'))
- residual: float32 [64, 1048576], P(None, ('region', 'layer'))
- mech_temps: float32 [4096, 8192], P(('region', 'layer'))
The draws below stay inside these ranges and needn't reach their ends.
Inputs may be any that keep to these rules, and one draw needn't show every extreme that they name: `block_entries`: dense blocks of the conduction operator: the diagonal block of each block row carries the node's own coupling on its diagonal. `die_owner`: among the 512 rows of one device, at most 128 name the same owner, and in some devices exactly 128 do.
All inputs are finite; a program needn't handle non-finite values.
Results may differ from the reference program's by a relative error of at most 0.0003.
Values sent between devices are 32-bit elements; how exact they have to be, the bound alone decides.
No kernel may reach another device: no remote copies, remote signals or barrier semaphores. Data moves between devices by JAX's collectives and lax.ppermute only.
A program may use at most 128 MiB of HBM per device.

```python
import math
import jax
import jax.numpy as jnp
import numpy as np
from jax import lax

BLOCK = 64
RHS = 64
COUPLED = 7
BLK_DEV = 64
DIE_ROWS = 512
SLOTS = 128
FACES = 8
BLOCKS_ALL = 16384
NODES = 1048576
N_REGION = 16
N_LAYER = 16


def draw_block_entries(key, part):
    first_key, second_key = jax.random.split(key)
    spread = 1.2 / BLOCK
    shape_all = (BLOCKS_ALL, COUPLED, BLOCK * BLOCK)
    entries = jax.random.uniform(first_key, shape_all, jnp.float32, -spread, spread)
    diag_vals = jax.random.uniform(second_key, (BLOCKS_ALL, 1, BLOCK), jnp.float32, 1.0, 2.0)
    spread_diag = jnp.repeat(diag_vals, BLOCK, axis=2)
    position = jnp.arange(BLOCK * BLOCK)
    on_diag = (position // BLOCK == position % BLOCK)[None, :] & (jnp.arange(COUPLED)[:, None] == 0)
    return entries + jnp.where(on_diag[None, :, :], spread_diag, jnp.float32(0.0))


def draw_right_side(key, part):
    keys = jax.random.split(key, 3)
    node_scale = jnp.exp(jax.random.uniform(keys[0], (1, NODES), jnp.float32, math.log(0.3), math.log(3.0)))
    column_scale = jnp.exp(jax.random.uniform(keys[1], (RHS, 1), jnp.float32, math.log(0.5), math.log(2.0)))
    ramp = 1.0 + 2.0 * jnp.arange(NODES, dtype=jnp.float32)[None, :] / jnp.float32(NODES - 1)
    base = jnp.clip(jax.random.normal(keys[2], (RHS, NODES), jnp.float32), -4.0, 4.0)
    return base * node_scale * ramp * column_scale


def place_ends(result, key, low, high):
    longest = result.shape.index(max(result.shape))
    spots = []
    for shift in (0, 1):
        where = [jax.random.randint(jax.random.fold_in(key, axis), (), 0, length) for axis, length in enumerate(result.shape)]
        where[longest] = (where[longest] + shift) % result.shape[longest]
        spots.append(tuple(where))
    return result.at[spots[0]].set(low).at[spots[1]].set(high)


def deal_out(stream_key, own, number, rows, amount, top, reach, lean):
    sequence = jax.random.permutation(stream_key, amount)
    packed, usual = load_shares(amount, rows * top, reach, lean, True), load_shares(amount, rows * top, reach, lean, False)
    places = jnp.arange(amount)

    def named(lengths, offset_by):
        used = int((lengths > 0).sum())
        fixed = max(1, used // 4)
        shifted = fixed + (places - fixed + offset_by * (used - fixed)) % max(1, amount - fixed)
        return jnp.zeros((amount,), jnp.int32).at[sequence[jnp.where(places < fixed, places, shifted)]].set(jnp.asarray(lengths, jnp.int32))

    lengths = jnp.where(number % 4 == 0, named(packed, number // 4), named(usual, number - number // 4 - 1))
    mixed = jax.random.permutation(jax.random.fold_in(own, 3), amount)
    giver, sink = mixed[0:amount // 2 * 2:2], mixed[1:amount // 2 * 2:2]
    room = jnp.minimum(lengths[giver] - 1, reach - lengths[sink]) // 2
    room = jnp.where((giver == sequence[0]) | (sink == sequence[0]) | (lengths[sink] == 0), 0, jnp.maximum(room, 0))
    shifted = jax.random.randint(jax.random.fold_in(own, 4), (amount // 2,), 0, 1 << 20) % (room + 1)
    lengths = lengths.at[giver].add(-shifted).at[sink].add(shifted)
    labels = jnp.searchsorted(jnp.cumsum(lengths), jnp.arange(rows * top), side="right").astype(jnp.int32)
    table = labels.reshape(top, rows).T
    table = table[jax.random.permutation(jax.random.fold_in(own, 1), rows)]
    offset_by = jax.random.randint(jax.random.fold_in(own, 2), (rows, 1), 0, top)
    return jnp.take_along_axis(table, (jnp.arange(top)[None, :] + offset_by) % top, axis=1)


def load_shares(amount, total, most, slope, full):
    portions = [(1 << 20) // math.isqrt(rank ** slope) + 1 for rank in range(1, amount + 1)]
    largest = most if full else min(most, max(-(-total // amount), total * portions[0] // sum(portions)))
    least = 1 if total - largest >= amount - 1 else 0
    given, rest = [largest] + [least] * (amount - 1), total - largest - least * (amount - 1)
    while rest > 0:
        movable = [i for i in range(1, amount) if given[i] < largest] or [i for i in range(1, amount) if given[i] < most]
        mass, left = sum([portions[i] for i in movable]), rest
        for i in movable:
            addition = min(most - given[i], max(1, left * portions[i] // mass), rest)
            given[i] = given[i] + addition
            rest = rest - addition
    return np.array(given)


def setup_inputs(seed: int = 0) -> dict:
    key_of = jax.random.split(jax.random.key(seed), 7)
    right_side = draw_right_side(jax.random.fold_in(key_of[6], 71), 0)
    block_entries = draw_block_entries(jax.random.fold_in(key_of[6], 71), 0)
    neighbours = place_ends(jax.random.randint(key_of[2], (BLOCKS_ALL, COUPLED - 1), 0, BLK_DEV + 4 * FACES), jax.random.fold_in(key_of[2], 1), 0, (BLK_DEV + 4 * FACES) - 1).astype(jnp.int32)
    face_rows = place_ends(jax.random.randint(key_of[3], (N_REGION * N_LAYER * 4, FACES), 0, BLK_DEV), jax.random.fold_in(key_of[3], 1), 0, BLK_DEV - 1).astype(jnp.int32)
    die_owner_keys = jax.random.split(jax.random.fold_in(key_of[4], 1), (N_REGION * N_LAYER * DIE_ROWS) // DIE_ROWS)
    die_owner_turns = jax.random.permutation(jax.random.fold_in(key_of[4], 3), (N_REGION * N_LAYER * DIE_ROWS) // DIE_ROWS)
    die_owner = jax.vmap(lambda own, number: deal_out(jax.random.fold_in(key_of[4], 2), own, number, DIE_ROWS, N_LAYER, 1, SLOTS, 2))(die_owner_keys, die_owner_turns).reshape((N_REGION * N_LAYER * DIE_ROWS, 1))
    die_node = place_ends(jax.random.randint(key_of[5], (N_REGION * N_LAYER * DIE_ROWS,), 0, BLK_DEV * BLOCK), jax.random.fold_in(key_of[5], 1), 0, (BLK_DEV * BLOCK) - 1).astype(jnp.int32)
    return dict(right_side=right_side, block_entries=block_entries, neighbours=neighbours, face_rows=face_rows, die_owner=die_owner, die_node=die_node)


def exact_dot(left, right):
    return jnp.dot(left.astype(jnp.float32), right.astype(jnp.float32), precision=lax.Precision.HIGHEST, preferred_element_type=jnp.float32)

def chol_solve(matrix, target):
    lower_factor = jnp.linalg.cholesky(matrix)
    halfway = lax.linalg.triangular_solve(lower_factor, target, left_side=True, lower=True)
    return lax.linalg.triangular_solve(lower_factor, halfway, left_side=True, lower=True, transpose_a=True)

def place_rows(values_rows, owners):
    owner_hits = (owners[:, None] == jnp.arange(N_LAYER, dtype=jnp.int32)[None, :]).astype(jnp.int32)
    earlier_hits = jnp.cumsum(owner_hits, axis=0, dtype=jnp.int32) - owner_hits
    rank_index = jnp.sum(earlier_hits * owner_hits, axis=1, dtype=jnp.int32)
    slot_index = owners * SLOTS + rank_index
    empty_rows = jnp.zeros((N_LAYER * SLOTS, values_rows.shape[1]), values_rows.dtype)
    return empty_rows.at[slot_index].set(values_rows)

def peer_tables():
    device_count = N_REGION * N_LAYER
    device_ids = np.arange(device_count)
    region_ids = device_ids // N_LAYER
    layer_ids = device_ids % N_LAYER
    near_idx = (region_ids ^ 1) * N_LAYER + layer_ids
    far_idx = (region_ids ^ N_REGION // 2) * N_LAYER + layer_ids
    below_idx = region_ids * N_LAYER + np.maximum(layer_ids - 1, 0)
    above_idx = region_ids * N_LAYER + np.minimum(layer_ids + 1, N_LAYER - 1)
    has_below = (layer_ids > 0).astype(np.float32)
    has_above = (layer_ids < N_LAYER - 1).astype(np.float32)
    return (jnp.asarray(near_idx, dtype=jnp.int32), jnp.asarray(far_idx, dtype=jnp.int32), jnp.asarray(below_idx, dtype=jnp.int32), jnp.asarray(above_idx, dtype=jnp.int32), jnp.asarray(has_below, dtype=jnp.float32), jnp.asarray(has_above, dtype=jnp.float32))

def apply_all(field, block_entries, neighbours, face_rows):
    device_count = N_REGION * N_LAYER
    near_idx, far_idx, below_idx, above_idx, has_below, has_above = peer_tables()
    tiles = field.reshape(RHS, device_count, BLK_DEV, BLOCK).transpose(1, 0, 2, 3)
    face_list = face_rows.reshape(device_count, 4 * FACES)

    def pick_faces(tile_set, chosen):
        return jnp.take(tile_set, chosen, axis=1)
    outgoing = jax.vmap(pick_faces)(tiles, face_list).reshape(device_count, RHS, 4, FACES, BLOCK)
    near_rows = outgoing[near_idx, :, 0]
    far_rows = outgoing[far_idx, :, 1]
    below_rows = outgoing[below_idx, :, 2] * has_below[:, None, None, None]
    above_rows = outgoing[above_idx, :, 3] * has_above[:, None, None, None]
    tile_mats = block_entries.reshape(device_count, BLK_DEV, COUPLED, BLOCK, BLOCK)
    neighbour_sets = neighbours.reshape(device_count, BLK_DEV * (COUPLED - 1))

    def device_product(inputs):
        own_tiles, near_part, far_part, below_part, above_part, mats_here, chosen = inputs
        extended = jnp.concatenate([own_tiles, near_part, far_part, below_part, above_part], axis=1)
        picked = jnp.take(extended, chosen, axis=1).reshape(RHS, BLK_DEV, COUPLED - 1, BLOCK)
        columns = jnp.concatenate([own_tiles[:, :, None, :], picked], axis=2)
        return jnp.einsum('snkb,nkab->sna', columns, mats_here, precision=lax.Precision.HIGHEST)
    product = lax.map(device_product, (tiles, near_rows, far_rows, below_rows, above_rows, tile_mats, neighbour_sets))
    return product.transpose(1, 0, 2, 3).reshape(RHS, device_count * BLK_DEV * BLOCK)

def reference(right_side, block_entries, neighbours, face_rows, die_owner, die_node):
    device_count = N_REGION * N_LAYER
    resid_zero = right_side
    norm_zero = exact_dot(resid_zero, resid_zero.T)
    image_zero = apply_all(resid_zero, block_entries, neighbours, face_rows)
    curve_zero = exact_dot(resid_zero, image_zero.T)
    alpha_first = chol_solve(0.5 * (curve_zero + curve_zero.T), norm_zero)
    iterate_one = exact_dot(alpha_first.T, resid_zero)
    resid_one = resid_zero - exact_dot(alpha_first.T, image_zero)
    norm_one = exact_dot(resid_one, resid_one.T)
    beta_step = chol_solve(norm_zero, norm_one)
    direction = resid_one + exact_dot(beta_step.T, resid_zero)
    image_one = apply_all(direction, block_entries, neighbours, face_rows)
    curve_one = exact_dot(direction, image_one.T)
    alpha_second = chol_solve(0.5 * (curve_one + curve_one.T), norm_one)
    solution_field = iterate_one + exact_dot(alpha_second.T, direction)
    residual = resid_one - exact_dot(alpha_second.T, image_one)
    by_device = solution_field.reshape(RHS, device_count, BLK_DEV * BLOCK).transpose(1, 2, 0)

    def pick_rows(local_field, chosen):
        return jnp.take(local_field, chosen, axis=0)
    die_rows = jax.vmap(pick_rows)(by_device, die_node.reshape(device_count, DIE_ROWS))
    buffers = jax.vmap(place_rows)(die_rows, die_owner.reshape(device_count, DIE_ROWS))
    buffers = buffers.reshape(N_REGION, N_LAYER, N_LAYER, SLOTS * RHS).transpose(0, 2, 1, 3)
    mech_temps = buffers.reshape(N_REGION * N_LAYER * N_LAYER, SLOTS * RHS)
    return (solution_field, residual, mech_temps)
```

```python
import functools

import jax
import jax.numpy as jnp
from jax import lax
from jax.experimental import pallas as pl
from jax.experimental.pallas import tpu as pltpu
from jax.sharding import PartitionSpec as P

BLOCK = 64
RHS = 64
COUPLED = 7
BLK_DEV = 64
NODES_DEV = BLK_DEV * BLOCK
DIE_ROWS = 512
SLOTS = 128
FACES = 8
LANES = 128
STEP = 8
GRID = BLK_DEV // STEP
SHIFT = 1.5
BF16 = jnp.bfloat16
F32 = jnp.float32


def params(mib):
    return pltpu.CompilerParams(vmem_limit_bytes=mib * 1024 * 1024)


def cost(flops, moved):
    return pl.CostEstimate(flops=flops, bytes_accessed=moved, transcendentals=0)


def resident():
    return pl.BlockSpec(memory_space=pltpu.VMEM)


def smem():
    return pl.BlockSpec(memory_space=pltpu.SMEM)


def left_lanes(rows):
    return lax.broadcasted_iota(jnp.int32, (rows, LANES), 1) < RHS


def two_parts(doubled):
    lead = doubled.astype(BF16).astype(F32)
    return jnp.where(left_lanes(doubled.shape[0]), lead, doubled - lead).astype(BF16)


def emit_faces(face_rows, nodes_ref, face_refs):
    for side, face_ref in enumerate(face_refs):
        for face in range(FACES):
            start = pl.multiple_of(face_rows[side, face] * BLOCK, BLOCK)
            upper = nodes_ref[pl.ds(start, 32), :]
            lower = nodes_ref[pl.ds(start + 32, 32), :]
            face_ref[face * 32 : (face + 1) * 32, :] = jnp.where(left_lanes(32), upper, lower)


def field_kernel(face_rows, right_ref, parts_ref, nodes_ref, *face_refs):
    step = pl.program_id(0)
    for chunk in range(STEP * BLOCK // LANES):
        piece = right_ref[:, chunk * LANES : (chunk + 1) * LANES]
        doubled = jnp.concatenate([piece, piece], axis=0).T
        start = pl.multiple_of(step * STEP * BLOCK + chunk * LANES, LANES)
        nodes_ref[pl.ds(start, LANES), :] = doubled
        halves = two_parts(doubled)
        parts_ref[step * STEP + 2 * chunk] = halves[:BLOCK]
        parts_ref[step * STEP + 2 * chunk + 1] = halves[BLOCK:]

    @pl.when(step == GRID - 1)
    def _():
        emit_faces(face_rows, nodes_ref, face_refs)


def entries_kernel(raw_ref, mats_ref, rows_ref):
    step = pl.program_id(0)
    half = left_lanes(32)
    lane = lax.broadcasted_iota(jnp.int32, (32, LANES), 1)
    twice = 2 * lax.broadcasted_iota(jnp.int32, (32, LANES), 0)
    shift_even = jnp.where(lane == twice, SHIFT, 0.0)
    shift_odd = jnp.where(lane == twice + 1, SHIFT, 0.0)
    shift_odd = jnp.where(half, shift_odd, 0.0)
    shift_even = jnp.where(half, shift_even, 0.0)
    for k in range(COUPLED):
        for pair in range(32):
            rows_ref[pl.ds((k * 32 + pair) * STEP, STEP), :] = raw_ref[
                k, :, pair * LANES : (pair + 1) * LANES
            ]
    for item in range(STEP):
        for duo in range(4):
            first = rows_ref[pl.ds(2 * duo * 256 + item, 32, stride=STEP), :]
            if 2 * duo + 1 < COUPLED:
                second = rows_ref[pl.ds((2 * duo + 1) * 256 + item, 32, stride=STEP), :]
            else:
                second = jnp.zeros_like(first)
            even = jnp.where(half, first, pltpu.roll(second, RHS, 1))
            odd = jnp.where(half, pltpu.roll(first, RHS, 1), second)
            if duo == 0:
                even = even - shift_even
                odd = odd - shift_odd
            stacked = jnp.concatenate([even, odd], axis=0)
            lead = stacked.astype(BF16)
            rest = (stacked - lead.astype(F32)).astype(BF16)
            block = step * STEP + item
            mats_ref[block, :BLOCK, duo * LANES : (duo + 1) * LANES] = lead
            mats_ref[block, BLOCK:, duo * LANES : (duo + 1) * LANES] = rest


def fill_extended(parts_ref, received, extended_ref):
    extended_ref[:BLK_DEV] = parts_ref[...]
    half = left_lanes(32)
    for side, got_ref in enumerate(received):
        for face in range(FACES):
            packed = got_ref[face * 32 : (face + 1) * 32, :]
            turned = pltpu.roll(packed, RHS, 1)
            block = BLK_DEV + side * FACES + face
            extended_ref[block, :32] = two_parts(jnp.where(half, packed, turned))
            extended_ref[block, 32:] = two_parts(jnp.where(half, turned, packed))


def block_row(block, neighbours, mats_ref, extended_ref, nodes_ref):
    pieces = [extended_ref[block]]
    for k in range(COUPLED - 1):
        pieces.append(extended_ref[neighbours[k, block]])
    pieces.append(pieces[0])
    product = jnp.dot(
        mats_ref[block], jnp.concatenate(pieces, axis=0), preferred_element_type=F32
    )
    folded = product[:BLOCK] + product[BLOCK:]
    doubled = folded + pltpu.roll(folded, RHS, 1)
    start = pl.multiple_of(block * BLOCK, BLOCK)
    nodes_ref[pl.ds(start, 32, stride=2), :] = doubled[:32]
    nodes_ref[pl.ds(start + 1, 32, stride=2), :] = doubled[32:]
    return nodes_ref[pl.ds(start, BLOCK), :]


def first_kernel(
    neighbours, face_rows, mats_ref, parts_ref, own_ref, near, far, below, above,
    image_ref, both_ref, out0, out1, out2, out3, extended_ref, nodes_ref,
):
    fill_extended(parts_ref, (near, far, below, above), extended_ref)

    def group(step, carry):
        for item in range(STEP):
            block = step * STEP + item
            doubled = block_row(block, neighbours, mats_ref, extended_ref, nodes_ref)
            image_ref[block] = two_parts(doubled)
            rows = pl.ds(pl.multiple_of(block * BLOCK, BLOCK), BLOCK)
            both_ref[rows, :] = jnp.where(left_lanes(BLOCK), own_ref[rows, :], doubled)
        return carry

    lax.fori_loop(0, GRID, group, 0)
    emit_faces(face_rows, nodes_ref, (out0, out1, out2, out3))


def gram_of(left, right):
    return lax.dot_general(left, right, (((0,), (0,)), ((), ())), preferred_element_type=F32)


def quarter_sum(grid):
    tall = grid[:RHS] + grid[RHS:]
    return tall + pltpu.roll(tall, RHS, 1)


def rows_of(ref, step):
    first = pl.multiple_of(step * STEP, STEP)
    return ref[pl.ds(first, STEP)].reshape(STEP * BLOCK, LANES)


def gram_kernel(field_ref, image_ref, out_ref, wide_acc, acc_ref):
    wide_acc[...] = jnp.zeros_like(wide_acc)
    acc_ref[...] = jnp.zeros_like(acc_ref)

    def group(step, carry):
        field = rows_of(field_ref, step)
        image = rows_of(image_ref, step)
        wide_acc[...] += gram_of(field, jnp.concatenate([field, image], axis=1))
        acc_ref[...] += gram_of(image, image)
        return carry

    lax.fori_loop(0, GRID, group, 0)
    out_ref[:RHS, :] = quarter_sum(wide_acc[:, :LANES])
    out_ref[RHS:LANES, :] = quarter_sum(wide_acc[:, LANES:])
    out_ref[LANES:, :] = quarter_sum(acc_ref[...])


def second_kernel(
    neighbours, mats_ref, parts_ref, near, far, below, above, field_ref, gram_ref,
    image_ref, sums_ref, extended_ref, nodes_ref, acc_ref,
):
    fill_extended(parts_ref, (near, far, below, above), extended_ref)
    acc_ref[...] = jnp.zeros_like(acc_ref)

    def group(step, carry):
        for item in range(STEP):
            block = step * STEP + item
            doubled = block_row(block, neighbours, mats_ref, extended_ref, nodes_ref)
            image_ref[block] = two_parts(doubled)
        joined = jnp.concatenate([rows_of(field_ref, step), rows_of(parts_ref, step)], axis=1)
        acc_ref[...] += gram_of(joined, rows_of(image_ref, step))
        return carry

    lax.fori_loop(0, GRID, group, 0)
    pack_sums(
        gram_ref[:RHS, :],
        gram_ref[RHS:LANES, :],
        gram_ref[LANES:, :],
        quarter_sum(acc_ref[:LANES]),
        quarter_sum(acc_ref[LANES:]),
        sums_ref,
    )


def pack_sums(norm, curve, image_norm, far_field, far_image, sums_ref):
    half = left_lanes(RHS)
    row = lax.broadcasted_iota(jnp.int32, (RHS, LANES), 0)
    col = lax.broadcasted_iota(jnp.int32, (RHS, LANES), 1)
    col = jnp.where(half, col, col - RHS)
    upper = row <= col
    diagonal = jnp.sum(jnp.where(row == col, image_norm, 0.0), axis=0, keepdims=True)
    last = jnp.where(row == RHS - 2, diagonal[:, RHS - 1 : RHS], diagonal)
    square = far_image[:, :RHS]
    balanced = 0.5 * (square + square.T)
    balanced = jnp.concatenate([balanced, balanced], axis=1)
    packed = jnp.where(upper, balanced, last)
    sums_ref[:RHS, :] = jnp.where(half, jnp.where(upper, norm, image_norm), curve)
    sums_ref[RHS:, :] = jnp.where(half, far_field, packed)


def unpack_sums(sums_ref):
    pair = sums_ref[:RHS, :RHS]
    curve = sums_ref[:RHS, RHS:]
    far_field = sums_ref[RHS:, :RHS]
    packed = sums_ref[RHS:, RHS:]
    row = lax.broadcasted_iota(jnp.int32, (RHS, RHS), 0)
    col = lax.broadcasted_iota(jnp.int32, (RHS, RHS), 1)
    pair_t = pair.T
    packed_t = packed.T
    norm = jnp.where(row <= col, pair, pair_t)
    lanes = lax.broadcasted_iota(jnp.int32, (1, RHS), 1)
    diagonal = jnp.where(
        lanes == RHS - 1, packed[RHS - 2 : RHS - 1, :1], packed[RHS - 1 : RHS, :]
    )
    image_norm = jnp.where(row > col, pair, pair_t)
    image_norm = jnp.where(row == col, diagonal, image_norm)
    far_image = jnp.where(row <= col, packed, packed_t)
    return norm, curve, image_norm, far_field, far_image


def relay_kernel(owners, die_node, both_ref, out_ref, counts):
    out_ref[...] = jnp.zeros_like(out_ref)
    for owner in range(16):
        counts[owner] = owner * SLOTS

    def move(row, carry):
        owner = owners[row]
        slot = counts[owner]
        counts[owner] = slot + 1
        out_ref[pl.ds(slot, 1), :] = both_ref[pl.ds(die_node[row], 1), :]
        return carry

    lax.fori_loop(0, DIE_ROWS, move, 0, unroll=8)


def mul(left, right):
    return jnp.dot(left, right, precision=lax.Precision.HIGHEST, preferred_element_type=F32)


def mul_t(left, right):
    return lax.dot_general(
        left,
        right,
        (((1,), (1,)), ((), ())),
        precision=lax.Precision.HIGHEST,
        preferred_element_type=F32,
    )


def eliminate(systems):
    row_id = lax.broadcasted_iota(jnp.int32, (RHS, 1), 0)
    for k in range(RHS):
        done = []
        for system in systems:
            pivot = system[k : k + 1, :] * (1.0 / system[k : k + 1, k : k + 1])
            done.append(jnp.where(row_id == k, pivot, system - system[:, k : k + 1] * pivot))
        systems = done
    return [system[:, RHS:] for system in systems]


def wide(left, right):
    return jnp.concatenate([left, right], axis=1)


def solve_steps(sums_ref):
    norm_zero, cross, image_norm, far_field, far_image = unpack_sums(sums_ref)
    eye = (
        lax.broadcasted_iota(jnp.int32, (RHS, RHS), 0)
        == lax.broadcasted_iota(jnp.int32, (RHS, RHS), 1)
    ).astype(F32)
    curve_zero = 0.5 * (cross + cross.T) + SHIFT * norm_zero
    alpha, norm_inverse = eliminate([wide(curve_zero, norm_zero), wide(norm_zero, eye)])
    alpha_t = alpha.T
    gram = jnp.concatenate([wide(norm_zero, cross), wide(cross.T, image_norm)], axis=0)
    shifted = jnp.concatenate([wide(cross, far_field), wide(image_norm, far_image)], axis=0)
    start = eye - SHIFT * alpha_t
    resid = wide(start, -alpha_t)
    norm_one = mul_t(mul(resid, gram), resid)
    mixed = start + mul(norm_inverse, norm_one).T
    direction = wide(mixed, -alpha_t)
    curve_one = mul_t(mul(direction, shifted + SHIFT * gram), direction)
    (alpha_two,) = eliminate([wide(0.5 * (curve_one + curve_one.T), norm_one)])
    second = mul(alpha_two.T, wide(mixed, alpha_t))
    gain, drop = second[:, :RHS], second[:, RHS:]
    keep = alpha_t + gain
    return keep, drop, start - SHIFT * gain, keep - SHIFT * drop


def halves_of(value):
    lead = value.astype(BF16)
    return lead, (value - lead.astype(F32)).astype(BF16)


def final_kernel(
    sums_ref, field_ref, image_ref, far_ref, solution_ref, residual_ref, coef_ref, weights_ref
):
    step = pl.program_id(0)

    @pl.when(step == 0)
    def _():
        keep, drop, left_over, taken = solve_steps(sums_ref)
        top = [wide(keep, keep), wide(-drop, -drop), jnp.zeros((RHS, LANES), F32)]
        low = [wide(left_over, left_over), wide(-taken, -taken), wide(drop, drop)]
        rows = jnp.concatenate(
            [jnp.concatenate(top, axis=1), jnp.concatenate(low, axis=1)], axis=0
        )
        lead, rest = halves_of(rows)
        weights_ref[:LANES] = lead
        weights_ref[LANES:] = rest
        coef_ref[...] = jnp.concatenate([keep.T, -drop.T], axis=0)

    basis = jnp.concatenate(
        [rows_of(ref, step) for ref in (field_ref, image_ref, far_ref)], axis=1
    )
    mixed = lax.dot_general(
        weights_ref[...], basis, (((1,), (1,)), ((), ())), preferred_element_type=F32
    )
    mixed = mixed[:LANES] + mixed[LANES:]
    solution_ref[...] = mixed[:RHS]
    residual_ref[...] = mixed[RHS:]


def owner_kernel(coef_ref, got_ref, out_ref):
    coef = coef_ref[...]
    none = jnp.zeros_like(coef)
    square = jnp.concatenate([wide(coef, none), wide(none, coef)], axis=0)
    weights = jnp.concatenate(halves_of(square), axis=1)
    for pack in range(8):
        pieces = []
        for pair in range(8 * pack, 8 * pack + 8):
            pieces.append(
                wide(
                    got_ref[pl.ds(2 * pair, 16, stride=SLOTS), :],
                    got_ref[pl.ds(2 * pair + 1, 16, stride=SLOTS), :],
                )
            )
        rows = jnp.concatenate(pieces, axis=0)
        lead, rest = halves_of(rows)
        product = jnp.dot(
            jnp.concatenate([lead, rest], axis=0), weights, preferred_element_type=F32
        )
        product = product[:LANES] + product[LANES:]
        product = product[:, :LANES] + product[:, LANES:]
        for at in range(8):
            pair = 8 * pack + at
            out_ref[:, pair * LANES : (pair + 1) * LANES] = product[16 * at : 16 * at + 16]


def swap(shard, axis, bit):
    return lax.ppermute(shard, axis, [(i, i ^ bit) for i in range(lax.axis_size(axis))])


def exchange(faces):
    count = lax.axis_size("layer")
    top = lax.axis_size("region") // 2
    near = swap(faces[0], "region", 1)
    far = swap(faces[1], "region", top)
    below = lax.ppermute(faces[2], "layer", [(i, i + 1) for i in range(count - 1)])
    above = lax.ppermute(faces[3], "layer", [(i + 1, i) for i in range(count - 1)])
    return near, far, below, above


def total(local):
    layers = lax.axis_size("layer")
    regions = lax.axis_size("region")
    parts = local.reshape(layers, LANES // layers, LANES)
    mine = jnp.sum(lax.all_to_all(parts, "layer", 0, 0, tiled=True), axis=0)
    copies = jnp.broadcast_to(mine[None], (regions,) + mine.shape)
    mine = jnp.sum(lax.all_to_all(copies, "region", 0, 0, tiled=True), axis=0)
    copies = jnp.broadcast_to(mine[None], (layers,) + mine.shape)
    return lax.all_to_all(copies, "layer", 0, 0, tiled=True).reshape(LANES, LANES)


PARTS = jax.ShapeDtypeStruct((BLK_DEV, BLOCK, LANES), BF16)
NODE_ROWS = jax.ShapeDtypeStruct((NODES_DEV, LANES), F32)
FACE = jax.ShapeDtypeStruct((FACES * 32, LANES), F32)
FIELD = jax.ShapeDtypeStruct((RHS, NODES_DEV), F32)
FIELD_STEP = pl.BlockSpec((RHS, STEP * BLOCK), lambda i: (0, i))


def on_device(right_side, block_entries, neighbours, face_rows, die_owner, die_node):
    owners = die_owner[:, 0]
    neighbours = neighbours.T
    entries = jnp.transpose(block_entries, (1, 0, 2))
    outcome = pl.pallas_call(
        field_kernel,
        grid=(GRID,),
        in_specs=[smem(), FIELD_STEP],
        out_specs=[resident()] * 6,
        out_shape=[PARTS, NODE_ROWS] + [FACE] * 4,
        compiler_params=params(8),
        cost_estimate=cost(1_000_000, 5_000_000),
        name="field",
    )(face_rows, right_side)
    field, own_rows, faces = outcome[0], outcome[1], outcome[2:]
    received = exchange(faces)
    mats = pl.pallas_call(
        entries_kernel,
        grid=(GRID,),
        in_specs=[pl.BlockSpec((COUPLED, STEP, BLOCK * BLOCK), lambda i: (0, i, 0))],
        out_specs=resident(),
        out_shape=jax.ShapeDtypeStruct((BLK_DEV, 2 * BLOCK, 4 * LANES), BF16),
        scratch_shapes=[pltpu.VMEM((COUPLED * 32 * STEP, LANES), F32)],
        compiler_params=params(8),
        cost_estimate=cost(10_000_000, 16_000_000),
        name="entries",
    )(entries)
    apply_scratch = [
        pltpu.VMEM((BLK_DEV + 4 * FACES, BLOCK, LANES), BF16),
        pltpu.VMEM((NODES_DEV, LANES), F32),
    ]
    outcome = pl.pallas_call(
        first_kernel,
        in_specs=[smem(), smem()] + [resident()] * 7,
        out_specs=[resident()] * 6,
        out_shape=[PARTS, NODE_ROWS] + [FACE] * 4,
        scratch_shapes=apply_scratch,
        compiler_params=params(8),
        cost_estimate=cost(1_000_000_000, 16_000_000),
        name="first_image",
    )(neighbours, face_rows, mats, field, own_rows, *received)
    image, both_rows, faces = outcome[0], outcome[1], outcome[2:]
    received = exchange(faces)
    outgoing = pl.pallas_call(
        relay_kernel,
        in_specs=[smem(), smem(), resident()],
        out_specs=resident(),
        out_shape=jax.ShapeDtypeStruct((16 * SLOTS, LANES), F32),
        scratch_shapes=[pltpu.SMEM((16,), jnp.int32)],
        compiler_params=params(8),
        cost_estimate=cost(1_000_000, 10_000_000),
        name="relay_rows",
    )(owners, die_node, both_rows)
    relayed = lax.all_to_all(
        outgoing.reshape(16, SLOTS, LANES), "layer", 0, 0, tiled=True
    ).reshape(16 * SLOTS, LANES)
    grams = pl.pallas_call(
        gram_kernel,
        in_specs=[resident()] * 2,
        out_specs=resident(),
        out_shape=jax.ShapeDtypeStruct((3 * RHS, LANES), F32),
        scratch_shapes=[pltpu.VMEM((LANES, 2 * LANES), F32), pltpu.VMEM((LANES, LANES), F32)],
        compiler_params=params(8),
        cost_estimate=cost(500_000_000, 2_000_000),
        name="near_grams",
    )(field, image)
    far_image, sums = pl.pallas_call(
        second_kernel,
        in_specs=[smem()] + [resident()] * 8,
        out_specs=[resident()] * 2,
        out_shape=[PARTS, jax.ShapeDtypeStruct((LANES, LANES), F32)],
        scratch_shapes=apply_scratch + [pltpu.VMEM((2 * LANES, LANES), F32)],
        compiler_params=params(8),
        cost_estimate=cost(1_000_000_000, 14_000_000),
        name="second_image",
    )(neighbours, mats, image, *received, field, grams)
    sums = total(sums)
    solution_field, residual, coef = pl.pallas_call(
        final_kernel,
        grid=(GRID,),
        in_specs=[resident()] * 4,
        out_specs=[FIELD_STEP, FIELD_STEP, resident()],
        out_shape=[FIELD, FIELD, jax.ShapeDtypeStruct((LANES, RHS), F32)],
        scratch_shapes=[pltpu.VMEM((2 * LANES, 3 * LANES), BF16)],
        compiler_params=params(8),
        cost_estimate=cost(500_000_000, 8_000_000),
        name="final",
    )(sums, field, image, far_image)
    mech_temps = pl.pallas_call(
        owner_kernel,
        in_specs=[resident()] * 2,
        out_specs=resident(),
        out_shape=jax.ShapeDtypeStruct((16, SLOTS * RHS), F32),
        compiler_params=params(8),
        cost_estimate=cost(100_000_000, 2_000_000),
        name="owner_rows",
    )(coef, relayed)
    return solution_field, residual, mech_temps


def solution(mesh):
    in_specs = (
        P(None, ("region", "layer")),
        P(("region", "layer"), None, None),
        P(("region", "layer"), None),
        P(("region", "layer"), None),
        P(("region", "layer"), None),
        P(("region", "layer")),
    )
    out_specs = (
        P(None, ("region", "layer")),
        P(None, ("region", "layer")),
        P(("region", "layer"), None),
    )
    return jax.shard_map(
        on_device, mesh=mesh, in_specs=in_specs, out_specs=out_specs, check_vma=False
    )
```

```python
import functools

import jax
import jax.numpy as jnp
from jax import lax
from jax.experimental import pallas as pl
from jax.experimental.pallas import tpu as pltpu
from jax.sharding import PartitionSpec as P

BLOCK = 64
RHS = 64
COUPLED = 7
BLK_DEV = 64
NODES_DEV = BLK_DEV * BLOCK
DIE_ROWS = 512
SLOTS = 128
FACES = 8
LANES = 128
STEP = 8
GRID = BLK_DEV // STEP
SHIFT = 1.5
BF16 = jnp.bfloat16
F32 = jnp.float32


def params(mib):
    return pltpu.CompilerParams(vmem_limit_bytes=mib * 1024 * 1024)


def in_hbm(array):
    return pltpu.with_memory_space_constraint(array, pltpu.HBM)


def cost(flops, moved):
    return pl.CostEstimate(flops=flops, bytes_accessed=moved, transcendentals=0)


def resident():
    return pl.BlockSpec(memory_space=pltpu.VMEM)


def smem():
    return pl.BlockSpec(memory_space=pltpu.SMEM)


def left_lanes(rows):
    return lax.broadcasted_iota(jnp.int32, (rows, LANES), 1) < RHS


def two_parts(doubled):
    lead = doubled.astype(BF16).astype(F32)
    return jnp.where(left_lanes(doubled.shape[0]), lead, doubled - lead).astype(BF16)


def emit_faces(face_rows, nodes_ref, face_refs):
    for side, face_ref in enumerate(face_refs):
        for face in range(FACES):
            start = pl.multiple_of(face_rows[side, face] * BLOCK, BLOCK)
            upper = nodes_ref[pl.ds(start, 32), :]
            lower = nodes_ref[pl.ds(start + 32, 32), :]
            face_ref[face * 32 : (face + 1) * 32, :] = jnp.where(left_lanes(32), upper, lower)


def columns_of(step):
    return pl.ds(pl.multiple_of(step * STEP * BLOCK, STEP * BLOCK), STEP * BLOCK)


def field_kernel(
    face_rows, right_hbm, parts_ref, turned_ref, nodes_ref, out0, out1, out2, out3, right_ref, sems
):
    copies = []
    for step in range(GRID):
        columns = pl.ds(step * STEP * BLOCK, STEP * BLOCK)
        copies.append(
            pltpu.make_async_copy(right_hbm.at[:, columns], right_ref.at[step], sems.at[step])
        )
        copies[step].start()
    for step in range(GRID):
        copies[step].wait()
        lead, rest = halves_of(right_ref[step])
        columns = slice(step * STEP * BLOCK, (step + 1) * STEP * BLOCK)
        turned_ref[:RHS, columns] = lead
        turned_ref[RHS:, columns] = rest
        for chunk in range(STEP * BLOCK // LANES):
            piece = right_ref[step, :, chunk * LANES : (chunk + 1) * LANES]
            doubled = jnp.concatenate([piece, piece], axis=0).T
            start = step * STEP * BLOCK + chunk * LANES
            nodes_ref[start : start + LANES, :] = doubled
            halves = two_parts(doubled)
            parts_ref[step * STEP + 2 * chunk] = halves[:BLOCK]
            parts_ref[step * STEP + 2 * chunk + 1] = halves[BLOCK:]
    emit_faces(face_rows, nodes_ref, (out0, out1, out2, out3))


def entries_kernel(raw_hbm, mats_ref, raw_ref, rows_ref, sems):
    half = left_lanes(32)
    lane = lax.broadcasted_iota(jnp.int32, (32, LANES), 1)
    twice = 2 * lax.broadcasted_iota(jnp.int32, (32, LANES), 0)
    shift_even = jnp.where(jnp.logical_and(half, lane == twice), SHIFT, 0.0)
    shift_odd = jnp.where(jnp.logical_and(half, lane == twice + 1), SHIFT, 0.0)

    def fetch(step):
        blocks = pl.ds(pl.multiple_of(step * STEP, STEP), STEP)
        return pltpu.make_async_copy(raw_hbm.at[:, blocks], raw_ref.at[step], sems.at[step])

    for step in range(GRID):
        fetch(step).start()

    def group(step, carry):
        fetch(step).wait()
        for k in range(COUPLED):
            for pair in range(32):
                rows_ref[pl.ds((k * 32 + pair) * STEP, STEP), :] = raw_ref[
                    step, k, :, pair * LANES : (pair + 1) * LANES
                ]
        for item in range(STEP):
            for duo in range(4):
                first = rows_ref[pl.ds(2 * duo * 256 + item, 32, stride=STEP), :]
                if 2 * duo + 1 < COUPLED:
                    second = rows_ref[pl.ds((2 * duo + 1) * 256 + item, 32, stride=STEP), :]
                else:
                    second = jnp.zeros_like(first)
                even = jnp.where(half, first, pltpu.roll(second, RHS, 1))
                odd = jnp.where(half, pltpu.roll(first, RHS, 1), second)
                if duo == 0:
                    even = even - shift_even
                    odd = odd - shift_odd
                lead, rest = halves_of(jnp.concatenate([even, odd], axis=0))
                block = step * STEP + item
                mats_ref[block, :BLOCK, duo * LANES : (duo + 1) * LANES] = lead
                mats_ref[block, BLOCK:, duo * LANES : (duo + 1) * LANES] = rest
        return carry

    lax.fori_loop(0, GRID, group, 0)


def fill_extended(parts_ref, received, extended_ref):
    extended_ref[:BLK_DEV] = parts_ref[...]
    half = left_lanes(32)
    for side, got_ref in enumerate(received):
        for face in range(FACES):
            packed = got_ref[face * 32 : (face + 1) * 32, :]
            turned = pltpu.roll(packed, RHS, 1)
            block = BLK_DEV + side * FACES + face
            extended_ref[block, :32] = two_parts(jnp.where(half, packed, turned))
            extended_ref[block, 32:] = two_parts(jnp.where(half, turned, packed))


def block_row(block, neighbours, mats_ref, extended_ref, nodes_ref):
    pieces = [extended_ref[block]]
    for k in range(COUPLED - 1):
        pieces.append(extended_ref[neighbours[k, block]])
    pieces.append(pieces[0])
    grid = product(mats_ref[block], jnp.concatenate(pieces, axis=0))
    folded = grid[:BLOCK] + grid[BLOCK:]
    doubled = folded + pltpu.roll(folded, RHS, 1)
    start = pl.multiple_of(block * BLOCK, BLOCK)
    nodes_ref[pl.ds(start, 32, stride=2), :] = doubled[:32]
    nodes_ref[pl.ds(start + 1, 32, stride=2), :] = doubled[32:]
    return nodes_ref[pl.ds(start, BLOCK), :]


def first_kernel(
    neighbours, face_rows, mats_ref, parts_ref, own_ref, near, far, below, above,
    image_ref, both_ref, out0, out1, out2, out3, extended_ref, nodes_ref,
):
    fill_extended(parts_ref, (near, far, below, above), extended_ref)

    def group(step, carry):
        for item in range(STEP):
            block = step * STEP + item
            doubled = block_row(block, neighbours, mats_ref, extended_ref, nodes_ref)
            image_ref[block] = two_parts(doubled)
            rows = pl.ds(pl.multiple_of(block * BLOCK, BLOCK), BLOCK)
            both_ref[rows, :] = jnp.where(left_lanes(BLOCK), own_ref[rows, :], doubled)
        return carry

    lax.fori_loop(0, GRID, group, 0)
    emit_faces(face_rows, nodes_ref, (out0, out1, out2, out3))


def quarter_sum(grid):
    tall = grid[:RHS] + grid[RHS:]
    return tall + pltpu.roll(tall, RHS, 1)


def rows_of(ref, step):
    first = pl.multiple_of(step * STEP, STEP)
    return ref[pl.ds(first, STEP)].reshape(STEP * BLOCK, LANES)


def product(left, right):
    return jnp.dot(left, right, preferred_element_type=F32)


def gram_kernel(turned_ref, field_ref, image_ref, out_ref, image_turned_ref, wide_acc, acc_ref):
    wide_acc[...] = jnp.zeros_like(wide_acc)
    acc_ref[...] = jnp.zeros_like(acc_ref)

    def group(step, carry):
        field = rows_of(field_ref, step)
        image = rows_of(image_ref, step)
        turned = image.T
        image_turned_ref[:, columns_of(step)] = turned
        wide_acc[...] += product(
            turned_ref[:, columns_of(step)], jnp.concatenate([field, image], axis=1)
        )
        acc_ref[...] += product(turned, image)
        return carry

    lax.fori_loop(0, GRID, group, 0)
    out_ref[:RHS, :] = quarter_sum(wide_acc[:, :LANES])
    out_ref[RHS:LANES, :] = quarter_sum(wide_acc[:, LANES:])
    out_ref[LANES:, :] = quarter_sum(acc_ref[...])


def second_kernel(
    neighbours, mats_ref, parts_ref, near, far, below, above, turned_ref, image_turned_ref,
    gram_ref, outgoing_ref, image_ref, sums_ref, extended_ref, nodes_ref, acc_ref,
):
    fill_extended(parts_ref, (near, far, below, above), extended_ref)
    acc_ref[...] = jnp.zeros_like(acc_ref)

    def group(step, carry):
        for item in range(STEP):
            block = step * STEP + item
            doubled = block_row(block, neighbours, mats_ref, extended_ref, nodes_ref)
            image_ref[block] = two_parts(doubled)
        columns = columns_of(step)
        both = jnp.concatenate([turned_ref[:, columns], image_turned_ref[:, columns]], axis=0)
        acc_ref[...] += product(both, rows_of(image_ref, step))
        return carry

    lax.fori_loop(0, GRID, group, 0)
    pack_sums(
        gram_ref[:RHS, :],
        gram_ref[RHS:LANES, :],
        gram_ref[LANES:, :],
        quarter_sum(acc_ref[:LANES]),
        quarter_sum(acc_ref[LANES:]),
        sums_ref,
    )


def pack_sums(norm, curve, image_norm, far_field, far_image, sums_ref):
    half = left_lanes(RHS)
    row = lax.broadcasted_iota(jnp.int32, (RHS, LANES), 0)
    col = lax.broadcasted_iota(jnp.int32, (RHS, LANES), 1)
    col = jnp.where(half, col, col - RHS)
    upper = row <= col
    diagonal = jnp.sum(jnp.where(row == col, image_norm, 0.0), axis=0, keepdims=True)
    last = jnp.where(row == RHS - 2, diagonal[:, RHS - 1 : RHS], diagonal)
    square = far_image[:, :RHS]
    balanced = 0.5 * (square + square.T)
    balanced = jnp.concatenate([balanced, balanced], axis=1)
    packed = jnp.where(upper, balanced, last)
    sums_ref[:RHS, :] = jnp.where(half, jnp.where(upper, norm, image_norm), curve)
    sums_ref[RHS:, :] = jnp.where(half, far_field, packed)


def unpack_sums(sums_ref):
    pair = sums_ref[:RHS, :RHS]
    curve = sums_ref[:RHS, RHS:]
    far_field = sums_ref[RHS:, :RHS]
    packed = sums_ref[RHS:, RHS:]
    row = lax.broadcasted_iota(jnp.int32, (RHS, RHS), 0)
    col = lax.broadcasted_iota(jnp.int32, (RHS, RHS), 1)
    pair_t = pair.T
    packed_t = packed.T
    norm = jnp.where(row <= col, pair, pair_t)
    lanes = lax.broadcasted_iota(jnp.int32, (1, RHS), 1)
    diagonal = jnp.where(
        lanes == RHS - 1, packed[RHS - 2 : RHS - 1, :1], packed[RHS - 1 : RHS, :]
    )
    image_norm = jnp.where(row > col, pair, pair_t)
    image_norm = jnp.where(row == col, diagonal, image_norm)
    far_image = jnp.where(row <= col, packed, packed_t)
    return norm, curve, image_norm, far_field, far_image


def relay_kernel(owners, die_node, both_ref, out_ref, counts):
    out_ref[...] = jnp.zeros_like(out_ref)
    for owner in range(16):
        counts[owner] = owner * SLOTS

    def move(row, carry):
        owner = owners[row]
        slot = counts[owner]
        counts[owner] = slot + 1
        out_ref[pl.ds(slot, 1), :] = both_ref[pl.ds(die_node[row], 1), :]
        return carry

    lax.fori_loop(0, DIE_ROWS, move, 0, unroll=8)


def mul(left, right):
    return jnp.dot(left, right, precision=lax.Precision.HIGHEST, preferred_element_type=F32)


def mul_t(left, right):
    return lax.dot_general(
        left,
        right,
        (((1,), (1,)), ((), ())),
        precision=lax.Precision.HIGHEST,
        preferred_element_type=F32,
    )


def eliminate(systems):
    tall = 8
    spread = (tall, LANES)
    sub = lax.broadcasted_iota(jnp.int32, spread, 0)
    grids = [[system[tall * r : tall * r + tall] for r in range(RHS // tall)] for system in systems]
    for pivot in range(RHS // tall):
        base = tall * pivot
        for tiles in grids:
            rows = tiles[pivot]
            entry = {
                (i, j): jnp.broadcast_to(rows[i : i + 1, base + j : base + j + 1], spread)
                for i in range(tall)
                for j in range(i + 1)
            }
            inverse, lower = [], {}
            for r in range(tall):
                inverse.append(1.0 / entry[r, r])
                for i in range(r + 1, tall):
                    lower[i, r] = entry[i, r] * inverse[r]
                    for j in range(r + 1, i + 1):
                        entry[i, j] = entry[i, j] - lower[i, r] * entry[j, r]
            solved = [jnp.broadcast_to(rows[i : i + 1, :], spread) for i in range(tall)]
            for i in range(tall):
                for j in range(i):
                    solved[i] = solved[i] - lower[i, j] * solved[j]
            for i in reversed(range(tall)):
                solved[i] = solved[i] * inverse[i]
                for j in range(i + 1, tall):
                    solved[i] = solved[i] - lower[j, i] * solved[j]
            for r in range(RHS // tall):
                if r == pivot:
                    continue
                old = tiles[r]
                fresh = old
                for i in range(tall):
                    fresh = fresh - old[:, base + i : base + i + 1] * solved[i]
                tiles[r] = fresh
            merged = solved[0]
            for i in range(1, tall):
                merged = jnp.where(sub == i, solved[i], merged)
            tiles[pivot] = merged
    return [jnp.concatenate(tiles, axis=0)[:, RHS:] for tiles in grids]


def wide(left, right):
    return jnp.concatenate([left, right], axis=1)


def solve_steps(sums_ref):
    norm_zero, cross, image_norm, far_field, far_image = unpack_sums(sums_ref)
    eye = (
        lax.broadcasted_iota(jnp.int32, (RHS, RHS), 0)
        == lax.broadcasted_iota(jnp.int32, (RHS, RHS), 1)
    ).astype(F32)
    curve_zero = 0.5 * (cross + cross.T) + SHIFT * norm_zero
    alpha, norm_inverse = eliminate([wide(curve_zero, norm_zero), wide(norm_zero, eye)])
    alpha_t = alpha.T
    gram = jnp.concatenate([wide(norm_zero, cross), wide(cross.T, image_norm)], axis=0)
    shifted = jnp.concatenate([wide(cross, far_field), wide(image_norm, far_image)], axis=0)
    start = eye - SHIFT * alpha_t
    resid = wide(start, -alpha_t)
    norm_one = mul_t(mul(resid, gram), resid)
    mixed = start + mul(norm_inverse, norm_one).T
    direction = wide(mixed, -alpha_t)
    curve_one = mul_t(mul(direction, shifted + SHIFT * gram), direction)
    (alpha_two,) = eliminate([wide(0.5 * (curve_one + curve_one.T), norm_one)])
    second = mul(alpha_two.T, wide(mixed, alpha_t))
    gain, drop = second[:, :RHS], second[:, RHS:]
    keep = alpha_t + gain
    return keep, drop, start - SHIFT * gain, keep - SHIFT * drop


def halves_of(value):
    lead = value.astype(BF16)
    return lead, (value - lead.astype(F32)).astype(BF16)


def final_kernel(
    sums_ref, turned_ref, image_turned_ref, far_ref, solution_ref, residual_ref, coef_ref, weights_ref
):
    step = pl.program_id(0)

    @pl.when(step == 0)
    def _():
        keep, drop, left_over, taken = solve_steps(sums_ref)
        top = [wide(keep, keep), wide(-drop, -drop), jnp.zeros((RHS, LANES), F32)]
        low = [wide(left_over, left_over), wide(-taken, -taken), wide(drop, drop)]
        rows = jnp.concatenate(
            [jnp.concatenate(top, axis=1), jnp.concatenate(low, axis=1)], axis=0
        )
        lead, rest = halves_of(rows)
        weights_ref[:LANES] = lead
        weights_ref[LANES:] = rest
        coef_ref[...] = jnp.concatenate([keep.T, -drop.T], axis=0)

    columns = columns_of(step)
    both = jnp.concatenate([turned_ref[:, columns], image_turned_ref[:, columns]], axis=0)
    mixed = product(weights_ref[:, : 2 * LANES], both) + lax.dot_general(
        weights_ref[:, 2 * LANES :],
        rows_of(far_ref, step),
        (((1,), (1,)), ((), ())),
        preferred_element_type=F32,
    )
    mixed = mixed[:LANES] + mixed[LANES:]
    solution_ref[...] = mixed[:RHS]
    residual_ref[...] = mixed[RHS:]


def owner_kernel(coef_ref, got_ref, out_ref):
    coef = coef_ref[...]
    none = jnp.zeros_like(coef)
    square = jnp.concatenate([wide(coef, none), wide(none, coef)], axis=0)
    weights = jnp.concatenate(halves_of(square), axis=1)
    for pack in range(8):
        pieces = []
        for pair in range(8 * pack, 8 * pack + 8):
            pieces.append(
                wide(
                    got_ref[pl.ds(2 * pair, 16, stride=SLOTS), :],
                    got_ref[pl.ds(2 * pair + 1, 16, stride=SLOTS), :],
                )
            )
        rows = jnp.concatenate(pieces, axis=0)
        lead, rest = halves_of(rows)
        grid = product(jnp.concatenate([lead, rest], axis=0), weights)
        grid = grid[:LANES] + grid[LANES:]
        grid = grid[:, :LANES] + grid[:, LANES:]
        for at in range(8):
            pair = 8 * pack + at
            out_ref[:, pair * LANES : (pair + 1) * LANES] = grid[16 * at : 16 * at + 16]


def swap(shard, axis, bit):
    return lax.ppermute(shard, axis, [(i, i ^ bit) for i in range(lax.axis_size(axis))])


def exchange(faces):
    count = lax.axis_size("layer")
    top = lax.axis_size("region") // 2
    near = swap(faces[0], "region", 1)
    far = swap(faces[1], "region", top)
    below = lax.ppermute(faces[2], "layer", [(i, i + 1) for i in range(count - 1)])
    above = lax.ppermute(faces[3], "layer", [(i + 1, i) for i in range(count - 1)])
    return near, far, below, above


def total(local):
    layers = lax.axis_size("layer")
    regions = lax.axis_size("region")
    parts = local.reshape(layers, LANES // layers, LANES)
    mine = jnp.sum(lax.all_to_all(parts, "layer", 0, 0, tiled=True), axis=0)
    copies = jnp.broadcast_to(mine[None], (regions,) + mine.shape)
    mine = jnp.sum(lax.all_to_all(copies, "region", 0, 0, tiled=True), axis=0)
    copies = jnp.broadcast_to(mine[None], (layers,) + mine.shape)
    return lax.all_to_all(copies, "layer", 0, 0, tiled=True).reshape(LANES, LANES)


TURNED = jax.ShapeDtypeStruct((LANES, NODES_DEV), BF16)
PARTS = jax.ShapeDtypeStruct((BLK_DEV, BLOCK, LANES), BF16)
NODE_ROWS = jax.ShapeDtypeStruct((NODES_DEV, LANES), F32)
FACE = jax.ShapeDtypeStruct((FACES * 32, LANES), F32)
FIELD = jax.ShapeDtypeStruct((RHS, NODES_DEV), F32)
FIELD_STEP = pl.BlockSpec((RHS, STEP * BLOCK), lambda i: (0, i))


def on_device(right_side, block_entries, neighbours, face_rows, die_owner, die_node):
    owners = in_hbm(die_owner[:, 0])
    die_node = in_hbm(die_node)
    neighbours = in_hbm(neighbours.T)
    face_rows = in_hbm(face_rows)
    entries = in_hbm(jnp.transpose(block_entries, (1, 0, 2)))
    right_side = in_hbm(right_side)
    outcome = pl.pallas_call(
        field_kernel,
        in_specs=[smem(), pl.BlockSpec(memory_space=pl.ANY)],
        out_specs=[resident()] * 7,
        out_shape=[PARTS, TURNED, NODE_ROWS] + [FACE] * 4,
        scratch_shapes=[
            pltpu.VMEM((GRID, RHS, STEP * BLOCK), F32),
            pltpu.SemaphoreType.DMA((GRID,)),
        ],
        compiler_params=params(8),
        cost_estimate=cost(1_000_000, 5_000_000),
        name="field",
    )(face_rows, right_side)
    field, turned, own_rows, faces = outcome[0], outcome[1], outcome[2], outcome[3:]
    received = exchange(faces)
    mats = pl.pallas_call(
        entries_kernel,
        in_specs=[pl.BlockSpec(memory_space=pl.ANY)],
        out_specs=resident(),
        out_shape=jax.ShapeDtypeStruct((BLK_DEV, 2 * BLOCK, 4 * LANES), BF16),
        scratch_shapes=[
            pltpu.VMEM((GRID, COUPLED, STEP, BLOCK * BLOCK), F32),
            pltpu.VMEM((COUPLED * 32 * STEP, LANES), F32),
            pltpu.SemaphoreType.DMA((GRID,)),
        ],
        compiler_params=params(12),
        cost_estimate=cost(10_000_000, 16_000_000),
        name="entries",
    )(entries)
    apply_scratch = [
        pltpu.VMEM((BLK_DEV + 4 * FACES, BLOCK, LANES), BF16),
        pltpu.VMEM((NODES_DEV, LANES), F32),
    ]
    outcome = pl.pallas_call(
        first_kernel,
        in_specs=[smem(), smem()] + [resident()] * 7,
        out_specs=[resident()] * 6,
        out_shape=[PARTS, NODE_ROWS] + [FACE] * 4,
        scratch_shapes=apply_scratch,
        compiler_params=params(8),
        cost_estimate=cost(1_000_000_000, 16_000_000),
        name="first_image",
    )(neighbours, face_rows, mats, field, own_rows, *received)
    image, both_rows, faces = outcome[0], outcome[1], outcome[2:]
    received = exchange(faces)
    outgoing = pl.pallas_call(
        relay_kernel,
        in_specs=[smem(), smem(), resident()],
        out_specs=resident(),
        out_shape=jax.ShapeDtypeStruct((16 * SLOTS, LANES), F32),
        scratch_shapes=[pltpu.SMEM((16,), jnp.int32)],
        compiler_params=params(8),
        cost_estimate=cost(1_000_000, 10_000_000),
        name="relay_rows",
    )(owners, die_node, both_rows)
    relayed = lax.all_to_all(
        outgoing.reshape(16, SLOTS, LANES), "layer", 0, 0, tiled=True
    ).reshape(16 * SLOTS, LANES)
    grams, image_turned = pl.pallas_call(
        gram_kernel,
        in_specs=[resident()] * 3,
        out_specs=[resident()] * 2,
        out_shape=[jax.ShapeDtypeStruct((3 * RHS, LANES), F32), TURNED],
        scratch_shapes=[pltpu.VMEM((LANES, 2 * LANES), F32), pltpu.VMEM((LANES, LANES), F32)],
        compiler_params=params(8),
        cost_estimate=cost(500_000_000, 2_000_000),
        name="near_grams",
    )(turned, field, image)
    far_image, sums = pl.pallas_call(
        second_kernel,
        in_specs=[smem()] + [resident()] * 9 + [pl.BlockSpec(memory_space=pl.ANY)],
        out_specs=[resident()] * 2,
        out_shape=[PARTS, jax.ShapeDtypeStruct((LANES, LANES), F32)],
        scratch_shapes=apply_scratch + [pltpu.VMEM((2 * LANES, LANES), F32)],
        compiler_params=params(8),
        cost_estimate=cost(1_000_000_000, 14_000_000),
        name="second_image",
    )(neighbours, mats, image, *received, turned, image_turned, grams, outgoing)
    sums = total(sums)
    solution_field, residual, coef = pl.pallas_call(
        final_kernel,
        grid=(GRID,),
        in_specs=[resident()] * 4,
        out_specs=[FIELD_STEP, FIELD_STEP, resident()],
        out_shape=[FIELD, FIELD, jax.ShapeDtypeStruct((LANES, RHS), F32)],
        scratch_shapes=[pltpu.VMEM((2 * LANES, 3 * LANES), BF16)],
        compiler_params=params(8),
        cost_estimate=cost(500_000_000, 8_000_000),
        name="final",
    )(sums, turned, image_turned, far_image)
    mech_temps = pl.pallas_call(
        owner_kernel,
        in_specs=[resident()] * 2,
        out_specs=resident(),
        out_shape=jax.ShapeDtypeStruct((16, SLOTS * RHS), F32),
        compiler_params=params(8),
        cost_estimate=cost(100_000_000, 2_000_000),
        name="owner_rows",
    )(coef, relayed)
    return solution_field, residual, mech_temps


def solution(mesh):
    in_specs = (
        P(None, ("region", "layer")),
        P(("region", "layer"), None, None),
        P(("region", "layer"), None),
        P(("region", "layer"), None),
        P(("region", "layer"), None),
        P(("region", "layer")),
    )
    out_specs = (
        P(None, ("region", "layer")),
        P(None, ("region", "layer")),
        P(("region", "layer"), None),
    )
    return jax.shard_map(
        on_device, mesh=mesh, in_specs=in_specs, out_specs=out_specs, check_vma=False
    )
```

```python
import functools

import jax
import jax.numpy as jnp
from jax import lax
from jax.experimental import pallas as pl
from jax.experimental.pallas import tpu as pltpu
from jax.sharding import PartitionSpec as P

BLOCK = 64
RHS = 64
COUPLED = 7
BLK_DEV = 64
NODES_DEV = BLK_DEV * BLOCK
DIE_ROWS = 512
SLOTS = 128
FACES = 8
LANES = 128
STEP = 8
GRID = BLK_DEV // STEP
SHIFT = 1.5
SAVE_ENDS = (47, 63)
BF16 = jnp.bfloat16
F32 = jnp.float32


def params(mib):
    return pltpu.CompilerParams(vmem_limit_bytes=mib * 1024 * 1024)


def far_memory():
    return pl.BlockSpec(memory_space=pltpu.HBM)


def in_hbm(array):
    return pltpu.with_memory_space_constraint(array, pltpu.HBM)


def cost(flops, moved):
    return pl.CostEstimate(flops=flops, bytes_accessed=moved, transcendentals=0)


def resident():
    return pl.BlockSpec(memory_space=pltpu.VMEM)


def smem():
    return pl.BlockSpec(memory_space=pltpu.SMEM)


def left_lanes(rows):
    return lax.broadcasted_iota(jnp.int32, (rows, LANES), 1) < RHS


def two_parts(doubled):
    lead = doubled.astype(BF16).astype(F32)
    return jnp.where(left_lanes(doubled.shape[0]), lead, doubled - lead).astype(BF16)


def emit_faces(face_rows, nodes_ref, face_refs):
    for side, face_ref in enumerate(face_refs):
        for face in range(FACES):
            start = pl.multiple_of(face_rows[side, face] * BLOCK, BLOCK)
            upper = nodes_ref[pl.ds(start, 32), :]
            lower = nodes_ref[pl.ds(start + 32, 32), :]
            face_ref[face * 32 : (face + 1) * 32, :] = jnp.where(left_lanes(32), upper, lower)


def columns_of(step):
    return slice(step * STEP * BLOCK, (step + 1) * STEP * BLOCK)


def field_kernel(
    face_rows, right_hbm, parts_ref, turned_ref, nodes_ref, out0, out1, out2, out3, right_ref, sems
):
    copies = []
    for step in range(GRID):
        columns = pl.ds(step * STEP * BLOCK, STEP * BLOCK)
        copies.append(
            pltpu.make_async_copy(right_hbm.at[:, columns], right_ref.at[step], sems.at[step])
        )
        copies[step].start()
    for step in range(GRID):
        copies[step].wait()
        lead, rest = halves_of(right_ref[step])
        columns = slice(step * STEP * BLOCK, (step + 1) * STEP * BLOCK)
        turned_ref[:RHS, columns] = lead
        turned_ref[RHS:, columns] = rest
        for chunk in range(STEP * BLOCK // LANES):
            piece = right_ref[step, :, chunk * LANES : (chunk + 1) * LANES]
            doubled = jnp.concatenate([piece, piece], axis=0).T
            start = step * STEP * BLOCK + chunk * LANES
            nodes_ref[start : start + LANES, :] = doubled
            halves = two_parts(doubled)
            parts_ref[step * STEP + 2 * chunk] = halves[:BLOCK]
            parts_ref[step * STEP + 2 * chunk + 1] = halves[BLOCK:]
    emit_faces(face_rows, nodes_ref, (out0, out1, out2, out3))


def entries_kernel(raw_hbm, mats_ref, raw_ref, rows_ref, sems):
    half = left_lanes(32)
    lane = lax.broadcasted_iota(jnp.int32, (32, LANES), 1)
    twice = 2 * lax.broadcasted_iota(jnp.int32, (32, LANES), 0)
    shift_even = jnp.where(jnp.logical_and(half, lane == twice), SHIFT, 0.0)
    shift_odd = jnp.where(jnp.logical_and(half, lane == twice + 1), SHIFT, 0.0)

    def fetch(step):
        blocks = pl.ds(step * STEP, STEP)
        return pltpu.make_async_copy(raw_hbm.at[:, blocks], raw_ref.at[step], sems.at[step])

    for step in range(GRID):
        fetch(step).start()

    for step in range(GRID):
        fetch(step).wait()
        for k in range(COUPLED):
            for pair in range(32):
                rows_ref[pl.ds((k * 32 + pair) * STEP, STEP), :] = raw_ref[
                    step, k, :, pair * LANES : (pair + 1) * LANES
                ]
        for item in range(STEP):
            for duo in range(4):
                first = rows_ref[pl.ds(2 * duo * 256 + item, 32, stride=STEP), :]
                if 2 * duo + 1 < COUPLED:
                    second = rows_ref[pl.ds((2 * duo + 1) * 256 + item, 32, stride=STEP), :]
                else:
                    second = jnp.zeros_like(first)
                even = jnp.where(half, first, pltpu.roll(second, RHS, 1))
                odd = jnp.where(half, pltpu.roll(first, RHS, 1), second)
                if duo == 0:
                    even = even - shift_even
                    odd = odd - shift_odd
                lead, rest = halves_of(jnp.concatenate([even, odd], axis=0))
                block = step * STEP + item
                mats_ref[block, :BLOCK, duo * LANES : (duo + 1) * LANES] = lead
                mats_ref[block, BLOCK:, duo * LANES : (duo + 1) * LANES] = rest


def fill_extended(parts_ref, received, extended_ref):
    extended_ref[:BLK_DEV] = parts_ref[...]
    half = left_lanes(32)
    for side, got_ref in enumerate(received):
        for face in range(FACES):
            packed = got_ref[face * 32 : (face + 1) * 32, :]
            turned = pltpu.roll(packed, RHS, 1)
            block = BLK_DEV + side * FACES + face
            extended_ref[block, :32] = two_parts(jnp.where(half, packed, turned))
            extended_ref[block, 32:] = two_parts(jnp.where(half, turned, packed))


def block_row(block, neighbours, mats_ref, extended_ref, nodes_ref):
    pieces = [extended_ref[block]]
    for k in range(COUPLED - 1):
        pieces.append(extended_ref[neighbours[k, block]])
    pieces.append(pieces[0])
    grid = product(mats_ref[block], jnp.concatenate(pieces, axis=0))
    folded = grid[:BLOCK] + grid[BLOCK:]
    doubled = folded + pltpu.roll(folded, RHS, 1)
    start = block * BLOCK
    nodes_ref[pl.ds(start, 32, stride=2), :] = doubled[:32]
    nodes_ref[pl.ds(start + 1, 32, stride=2), :] = doubled[32:]
    return nodes_ref[pl.ds(start, BLOCK), :]


def first_kernel(
    neighbours, face_rows, mats_ref, parts_ref, own_ref, near, far, below, above,
    image_ref, both_hbm, out0, out1, out2, out3, extended_ref, nodes_ref, both_ref, sem,
):
    def save(at):
        first = SAVE_ENDS[at - 1] + 1 if at else 0
        part = pl.ds(first * BLOCK, (SAVE_ENDS[at] + 1 - first) * BLOCK)
        return pltpu.make_async_copy(both_ref.at[part], both_hbm.at[part], sem.at[at])

    fill_extended(parts_ref, (near, far, below, above), extended_ref)
    for block in range(BLK_DEV):
        doubled = block_row(block, neighbours, mats_ref, extended_ref, nodes_ref)
        image_ref[block] = two_parts(doubled)
        rows = slice(block * BLOCK, (block + 1) * BLOCK)
        both_ref[rows, :] = jnp.where(left_lanes(BLOCK), own_ref[rows, :], doubled)
        if block in SAVE_ENDS:
            save(SAVE_ENDS.index(block)).start()
    emit_faces(face_rows, nodes_ref, (out0, out1, out2, out3))
    for at in range(len(SAVE_ENDS)):
        save(at).wait()


def quarter_sum(grid):
    tall = grid[:RHS] + grid[RHS:]
    return tall + pltpu.roll(tall, RHS, 1)


def rows_of(ref, step):
    return ref[step * STEP : (step + 1) * STEP].reshape(STEP * BLOCK, LANES)


def product(left, right):
    return jnp.dot(left, right, preferred_element_type=F32)


def gram_kernel(turned_ref, field_ref, image_ref, out_ref, image_turned_ref, wide_acc, acc_ref):
    wide_acc[...] = jnp.zeros_like(wide_acc)
    acc_ref[...] = jnp.zeros_like(acc_ref)
    for step in range(GRID):
        field = rows_of(field_ref, step)
        image = rows_of(image_ref, step)
        turned = image.T
        image_turned_ref[:, columns_of(step)] = turned
        wide_acc[...] += product(
            turned_ref[:, columns_of(step)], jnp.concatenate([field, image], axis=1)
        )
        acc_ref[...] += product(turned, image)
    out_ref[:RHS, :] = quarter_sum(wide_acc[:, :LANES])
    out_ref[RHS:LANES, :] = quarter_sum(wide_acc[:, LANES:])
    out_ref[LANES:, :] = quarter_sum(acc_ref[...])


def second_kernel(
    neighbours, mats_ref, parts_ref, near, far, below, above, turned_ref, image_turned_ref,
    gram_ref, image_hbm, sums_ref, extended_ref, nodes_ref, image_ref, acc_ref, sem,
):
    fill_extended(parts_ref, (near, far, below, above), extended_ref)
    acc_ref[...] = jnp.zeros_like(acc_ref)
    for block in range(BLK_DEV):
        doubled = block_row(block, neighbours, mats_ref, extended_ref, nodes_ref)
        image_ref[block] = two_parts(doubled)
    saving = pltpu.make_async_copy(image_ref, image_hbm, sem)
    saving.start()
    for step in range(GRID):
        columns = columns_of(step)
        both = jnp.concatenate([turned_ref[:, columns], image_turned_ref[:, columns]], axis=0)
        acc_ref[...] += product(both, rows_of(image_ref, step))
    pack_sums(
        gram_ref[:RHS, :],
        gram_ref[RHS:LANES, :],
        gram_ref[LANES:, :],
        quarter_sum(acc_ref[:LANES]),
        quarter_sum(acc_ref[LANES:]),
        sums_ref,
    )
    saving.wait()


def pack_sums(norm, curve, image_norm, far_field, far_image, sums_ref):
    half = left_lanes(RHS)
    row = lax.broadcasted_iota(jnp.int32, (RHS, LANES), 0)
    col = lax.broadcasted_iota(jnp.int32, (RHS, LANES), 1)
    col = jnp.where(half, col, col - RHS)
    upper = row <= col
    diagonal = jnp.sum(jnp.where(row == col, image_norm, 0.0), axis=0, keepdims=True)
    last = jnp.where(row == RHS - 2, diagonal[:, RHS - 1 : RHS], diagonal)
    square = far_image[:, :RHS]
    balanced = 0.5 * (square + square.T)
    balanced = jnp.concatenate([balanced, balanced], axis=1)
    packed = jnp.where(upper, balanced, last)
    sums_ref[:RHS, :] = jnp.where(half, jnp.where(upper, norm, image_norm), curve)
    sums_ref[RHS:, :] = jnp.where(half, far_field, packed)


def unpack_sums(sums_ref):
    pair = sums_ref[:RHS, :RHS]
    curve = sums_ref[:RHS, RHS:]
    far_field = sums_ref[RHS:, :RHS]
    packed = sums_ref[RHS:, RHS:]
    row = lax.broadcasted_iota(jnp.int32, (RHS, RHS), 0)
    col = lax.broadcasted_iota(jnp.int32, (RHS, RHS), 1)
    pair_t = pair.T
    packed_t = packed.T
    norm = jnp.where(row <= col, pair, pair_t)
    lanes = lax.broadcasted_iota(jnp.int32, (1, RHS), 1)
    diagonal = jnp.where(
        lanes == RHS - 1, packed[RHS - 2 : RHS - 1, :1], packed[RHS - 1 : RHS, :]
    )
    image_norm = jnp.where(row > col, pair, pair_t)
    image_norm = jnp.where(row == col, diagonal, image_norm)
    far_image = jnp.where(row <= col, packed, packed_t)
    return norm, curve, image_norm, far_field, far_image


def relay_kernel(owners, die_node, both_hbm, sums_hbm, out_ref, counts, both_ref, sem):
    fetch = pltpu.make_async_copy(both_hbm, both_ref, sem)
    fetch.start()
    out_ref[...] = jnp.zeros_like(out_ref)
    for owner in range(16):
        counts[owner] = owner * SLOTS
    fetch.wait()

    def move(row, carry):
        owner = owners[row]
        slot = counts[owner]
        counts[owner] = slot + 1
        out_ref[pl.ds(slot, 1), :] = both_ref[pl.ds(die_node[row], 1), :]
        return carry

    lax.fori_loop(0, DIE_ROWS, move, 0, unroll=8)


def mul(left, right):
    return jnp.dot(left, right, precision=lax.Precision.HIGHEST, preferred_element_type=F32)


def mul_t(left, right):
    return lax.dot_general(
        left,
        right,
        (((1,), (1,)), ((), ())),
        precision=lax.Precision.HIGHEST,
        preferred_element_type=F32,
    )


def eliminate(systems):
    tall = 8
    spread = (tall, LANES)
    sub = lax.broadcasted_iota(jnp.int32, spread, 0)
    grids = [[system[tall * r : tall * r + tall] for r in range(RHS // tall)] for system in systems]
    for pivot in range(RHS // tall):
        base = tall * pivot
        for tiles in grids:
            rows = tiles[pivot]
            entry = {
                (i, j): jnp.broadcast_to(rows[i : i + 1, base + j : base + j + 1], spread)
                for i in range(tall)
                for j in range(i + 1)
            }
            inverse, lower = [], {}
            for r in range(tall):
                inverse.append(1.0 / entry[r, r])
                for i in range(r + 1, tall):
                    lower[i, r] = entry[i, r] * inverse[r]
                    for j in range(r + 1, i + 1):
                        entry[i, j] = entry[i, j] - lower[i, r] * entry[j, r]
            solved = [jnp.broadcast_to(rows[i : i + 1, :], spread) for i in range(tall)]
            for i in range(tall):
                for j in range(i):
                    solved[i] = solved[i] - lower[i, j] * solved[j]
            for i in reversed(range(tall)):
                solved[i] = solved[i] * inverse[i]
                for j in range(i + 1, tall):
                    solved[i] = solved[i] - lower[j, i] * solved[j]
            for r in range(RHS // tall):
                if r == pivot:
                    continue
                old = tiles[r]
                fresh = old
                for i in range(tall):
                    fresh = fresh - old[:, base + i : base + i + 1] * solved[i]
                tiles[r] = fresh
            merged = solved[0]
            for i in range(1, tall):
                merged = jnp.where(sub == i, solved[i], merged)
            tiles[pivot] = merged
    return [jnp.concatenate(tiles, axis=0)[:, RHS:] for tiles in grids]


def wide(left, right):
    return jnp.concatenate([left, right], axis=1)


def solve_steps(sums_ref):
    norm_zero, cross, image_norm, far_field, far_image = unpack_sums(sums_ref)
    eye = (
        lax.broadcasted_iota(jnp.int32, (RHS, RHS), 0)
        == lax.broadcasted_iota(jnp.int32, (RHS, RHS), 1)
    ).astype(F32)
    curve_zero = 0.5 * (cross + cross.T) + SHIFT * norm_zero
    alpha, norm_inverse = eliminate([wide(curve_zero, norm_zero), wide(norm_zero, eye)])
    alpha_t = alpha.T
    gram = jnp.concatenate([wide(norm_zero, cross), wide(cross.T, image_norm)], axis=0)
    shifted = jnp.concatenate([wide(cross, far_field), wide(image_norm, far_image)], axis=0)
    start = eye - SHIFT * alpha_t
    resid = wide(start, -alpha_t)
    norm_one = mul_t(mul(resid, gram), resid)
    mixed = start + mul(norm_inverse, norm_one).T
    direction = wide(mixed, -alpha_t)
    curve_one = mul_t(mul(direction, shifted + SHIFT * gram), direction)
    (alpha_two,) = eliminate([wide(0.5 * (curve_one + curve_one.T), norm_one)])
    second = mul(alpha_two.T, wide(mixed, alpha_t))
    gain, drop = second[:, :RHS], second[:, RHS:]
    keep = alpha_t + gain
    return keep, drop, start - SHIFT * gain, keep - SHIFT * drop


def halves_of(value):
    lead = value.astype(BF16)
    return lead, (value - lead.astype(F32)).astype(BF16)


def final_kernel(
    sums_ref, turned_ref, image_turned_ref, far_hbm, solution_hbm, residual_hbm, coef_ref,
    far_ref, solution_ref, residual_ref, far_sem, sems,
):
    fetch = pltpu.make_async_copy(far_hbm, far_ref, far_sem)
    fetch.start()
    keep, drop, left_over, taken = solve_steps(sums_ref)
    top = [wide(keep, keep), wide(-drop, -drop), jnp.zeros((RHS, LANES), F32)]
    low = [wide(left_over, left_over), wide(-taken, -taken), wide(drop, drop)]
    rows = jnp.concatenate(
        [jnp.concatenate(top, axis=1), jnp.concatenate(low, axis=1)], axis=0
    )
    weights = jnp.concatenate(halves_of(rows), axis=0)
    coef_ref[...] = jnp.concatenate([keep.T, -drop.T], axis=0)
    fetch.wait()
    copies = []
    for step in range(GRID):
        columns = columns_of(step)
        both = jnp.concatenate([turned_ref[:, columns], image_turned_ref[:, columns]], axis=0)
        mixed = product(weights[:, : 2 * LANES], both) + lax.dot_general(
            weights[:, 2 * LANES :],
            rows_of(far_ref, step),
            (((1,), (1,)), ((), ())),
            preferred_element_type=F32,
        )
        mixed = mixed[:LANES] + mixed[LANES:]
        solution_ref[:, columns] = mixed[:RHS]
        residual_ref[:, columns] = mixed[RHS:]
        part = pl.ds(step * STEP * BLOCK, STEP * BLOCK)
        for at, (source, target) in enumerate(
            ((solution_ref, solution_hbm), (residual_ref, residual_hbm))
        ):
            copies.append(
                pltpu.make_async_copy(source.at[:, part], target.at[:, part], sems.at[at, step])
            )
            copies[-1].start()
    for copy in copies:
        copy.wait()


def owner_kernel(coef_ref, got_ref, out_ref):
    coef = coef_ref[...]
    none = jnp.zeros_like(coef)
    square = jnp.concatenate([wide(coef, none), wide(none, coef)], axis=0)
    weights = jnp.concatenate(halves_of(square), axis=1)
    for pack in range(8):
        pieces = []
        for pair in range(8 * pack, 8 * pack + 8):
            pieces.append(
                wide(
                    got_ref[pl.ds(2 * pair, 16, stride=SLOTS), :],
                    got_ref[pl.ds(2 * pair + 1, 16, stride=SLOTS), :],
                )
            )
        rows = jnp.concatenate(pieces, axis=0)
        lead, rest = halves_of(rows)
        grid = product(jnp.concatenate([lead, rest], axis=0), weights)
        grid = grid[:LANES] + grid[LANES:]
        grid = grid[:, :LANES] + grid[:, LANES:]
        for at in range(8):
            pair = 8 * pack + at
            out_ref[:, pair * LANES : (pair + 1) * LANES] = grid[16 * at : 16 * at + 16]


def swap(shard, axis, bit):
    return lax.ppermute(shard, axis, [(i, i ^ bit) for i in range(lax.axis_size(axis))])


def exchange(faces):
    count = lax.axis_size("layer")
    top = lax.axis_size("region") // 2
    near = swap(faces[0], "region", 1)
    far = swap(faces[1], "region", top)
    below = lax.ppermute(faces[2], "layer", [(i, i + 1) for i in range(count - 1)])
    above = lax.ppermute(faces[3], "layer", [(i + 1, i) for i in range(count - 1)])
    return near, far, below, above


def total(local):
    layers = lax.axis_size("layer")
    regions = lax.axis_size("region")
    parts = local.reshape(layers, LANES // layers, LANES)
    mine = jnp.sum(lax.all_to_all(parts, "layer", 0, 0, tiled=True), axis=0)
    copies = jnp.broadcast_to(mine[None], (regions,) + mine.shape)
    mine = jnp.sum(lax.all_to_all(copies, "region", 0, 0, tiled=True), axis=0)
    copies = jnp.broadcast_to(mine[None], (layers,) + mine.shape)
    return lax.all_to_all(copies, "layer", 0, 0, tiled=True).reshape(LANES, LANES)


TURNED = jax.ShapeDtypeStruct((LANES, NODES_DEV), BF16)
PARTS = jax.ShapeDtypeStruct((BLK_DEV, BLOCK, LANES), BF16)
NODE_ROWS = jax.ShapeDtypeStruct((NODES_DEV, LANES), F32)
FACE = jax.ShapeDtypeStruct((FACES * 32, LANES), F32)
FIELD = jax.ShapeDtypeStruct((RHS, NODES_DEV), F32)


def on_device(right_side, block_entries, neighbours, face_rows, die_owner, die_node):
    owners = in_hbm(die_owner[:, 0])
    die_node = in_hbm(die_node)
    neighbours = in_hbm(neighbours.T)
    face_rows = in_hbm(face_rows)
    entries = in_hbm(jnp.transpose(block_entries, (1, 0, 2)))
    right_side = in_hbm(right_side)
    outcome = pl.pallas_call(
        field_kernel,
        in_specs=[smem(), pl.BlockSpec(memory_space=pl.ANY)],
        out_specs=[resident()] * 7,
        out_shape=[PARTS, TURNED, NODE_ROWS] + [FACE] * 4,
        scratch_shapes=[
            pltpu.VMEM((GRID, RHS, STEP * BLOCK), F32),
            pltpu.SemaphoreType.DMA((GRID,)),
        ],
        compiler_params=params(8),
        cost_estimate=cost(1_000_000, 5_000_000),
        name="field",
    )(face_rows, right_side)
    field, turned, own_rows, faces = outcome[0], outcome[1], outcome[2], outcome[3:]
    received = exchange(faces)
    mats = pl.pallas_call(
        entries_kernel,
        in_specs=[pl.BlockSpec(memory_space=pl.ANY)],
        out_specs=resident(),
        out_shape=jax.ShapeDtypeStruct((BLK_DEV, 2 * BLOCK, 4 * LANES), BF16),
        scratch_shapes=[
            pltpu.VMEM((GRID, COUPLED, STEP, BLOCK * BLOCK), F32),
            pltpu.VMEM((COUPLED * 32 * STEP, LANES), F32),
            pltpu.SemaphoreType.DMA((GRID,)),
        ],
        compiler_params=params(12),
        cost_estimate=cost(10_000_000, 16_000_000),
        name="entries",
    )(entries)
    apply_scratch = [
        pltpu.VMEM((BLK_DEV + 4 * FACES, BLOCK, LANES), BF16),
        pltpu.VMEM((NODES_DEV, LANES), F32),
    ]
    outcome = pl.pallas_call(
        first_kernel,
        in_specs=[smem(), smem()] + [resident()] * 7,
        out_specs=[resident(), far_memory()] + [resident()] * 4,
        out_shape=[PARTS, pltpu.HBM(NODE_ROWS.shape, F32)] + [FACE] * 4,
        scratch_shapes=apply_scratch
        + [pltpu.VMEM((NODES_DEV, LANES), F32), pltpu.SemaphoreType.DMA((len(SAVE_ENDS),))],
        compiler_params=params(8),
        cost_estimate=cost(1_000_000_000, 16_000_000),
        name="first_image",
    )(neighbours, face_rows, mats, field, own_rows, *received)
    image, both_rows, faces = outcome[0], outcome[1], outcome[2:]
    received = exchange(faces)
    grams, image_turned = pl.pallas_call(
        gram_kernel,
        in_specs=[resident()] * 3,
        out_specs=[resident()] * 2,
        out_shape=[jax.ShapeDtypeStruct((3 * RHS, LANES), F32), TURNED],
        scratch_shapes=[pltpu.VMEM((LANES, 2 * LANES), F32), pltpu.VMEM((LANES, LANES), F32)],
        compiler_params=params(8),
        cost_estimate=cost(500_000_000, 2_000_000),
        name="near_grams",
    )(turned, field, image)
    far_image, local_sums = pl.pallas_call(
        second_kernel,
        in_specs=[smem()] + [resident()] * 9,
        out_specs=[far_memory(), resident()],
        out_shape=[
            pltpu.HBM(PARTS.shape, BF16),
            jax.ShapeDtypeStruct((LANES, LANES), F32),
        ],
        scratch_shapes=apply_scratch
        + [
            pltpu.VMEM(PARTS.shape, BF16),
            pltpu.VMEM((2 * LANES, LANES), F32),
            pltpu.SemaphoreType.DMA,
        ],
        compiler_params=params(8),
        cost_estimate=cost(1_000_000_000, 14_000_000),
        name="second_image",
    )(neighbours, mats, image, *received, turned, image_turned, grams)
    outgoing = pl.pallas_call(
        relay_kernel,
        in_specs=[smem(), smem(), far_memory(), pl.BlockSpec(memory_space=pl.ANY)],
        out_specs=resident(),
        out_shape=jax.ShapeDtypeStruct((16 * SLOTS, LANES), F32),
        scratch_shapes=[
            pltpu.SMEM((16,), jnp.int32),
            pltpu.VMEM((NODES_DEV, LANES), F32),
            pltpu.SemaphoreType.DMA,
        ],
        compiler_params=params(8),
        cost_estimate=cost(1_000_000, 10_000_000),
        name="relay_rows",
    )(owners, die_node, in_hbm(both_rows), local_sums)
    relayed = lax.all_to_all(
        outgoing.reshape(16, SLOTS, LANES), "layer", 0, 0, tiled=True
    ).reshape(16 * SLOTS, LANES)
    sums = total(local_sums)
    solution_field, residual, coef = pl.pallas_call(
        final_kernel,
        in_specs=[resident()] * 3 + [far_memory()],
        out_specs=[far_memory()] * 2 + [resident()],
        out_shape=[FIELD, FIELD, jax.ShapeDtypeStruct((LANES, RHS), F32)],
        scratch_shapes=[
            pltpu.VMEM(PARTS.shape, BF16),
            pltpu.VMEM(FIELD.shape, F32),
            pltpu.VMEM(FIELD.shape, F32),
            pltpu.SemaphoreType.DMA,
            pltpu.SemaphoreType.DMA((2, GRID)),
        ],
        compiler_params=params(8),
        cost_estimate=cost(500_000_000, 8_000_000),
        name="final",
    )(sums, turned, image_turned, in_hbm(far_image))
    mech_temps = pl.pallas_call(
        owner_kernel,
        in_specs=[resident()] * 2,
        out_specs=resident(),
        out_shape=jax.ShapeDtypeStruct((16, SLOTS * RHS), F32),
        compiler_params=params(8),
        cost_estimate=cost(100_000_000, 2_000_000),
        name="owner_rows",
    )(coef, relayed)
    return solution_field, residual, mech_temps


def solution(mesh):
    in_specs = (
        P(None, ("region", "layer")),
        P(("region", "layer"), None, None),
        P(("region", "layer"), None),
        P(("region", "layer"), None),
        P(("region", "layer"), None),
        P(("region", "layer")),
    )
    out_specs = (
        P(None, ("region", "layer")),
        P(None, ("region", "layer")),
        P(("region", "layer"), None),
    )
    return jax.shard_map(
        on_device, mesh=mesh, in_specs=in_specs, out_specs=out_specs, check_vma=False
    )
```

```python
import functools

import jax
import jax.numpy as jnp
from jax import lax
from jax.experimental import pallas as pl
from jax.experimental.pallas import tpu as pltpu
from jax.sharding import PartitionSpec as P

BLOCK = 64
RHS = 64
COUPLED = 7
BLK_DEV = 64
NODES_DEV = BLK_DEV * BLOCK
DIE_ROWS = 512
SLOTS = 128
FACES = 8
LANES = 128
STEP = 8
GRID = BLK_DEV // STEP
SHIFT = 1.5
BF16 = jnp.bfloat16
F32 = jnp.float32


def params(mib):
    return pltpu.CompilerParams(vmem_limit_bytes=mib * 1024 * 1024)


def far_memory():
    return pl.BlockSpec(memory_space=pltpu.HBM)


def in_hbm(array):
    return pltpu.with_memory_space_constraint(array, pltpu.HBM)


def cost(flops, moved):
    return pl.CostEstimate(flops=flops, bytes_accessed=moved, transcendentals=0)


def resident():
    return pl.BlockSpec(memory_space=pltpu.VMEM)


def smem():
    return pl.BlockSpec(memory_space=pltpu.SMEM)


def left_lanes(rows):
    return lax.broadcasted_iota(jnp.int32, (rows, LANES), 1) < RHS


def two_parts(doubled):
    lead = doubled.astype(BF16).astype(F32)
    return jnp.where(left_lanes(doubled.shape[0]), lead, doubled - lead).astype(BF16)


def emit_faces(face_rows, odd, nodes_ref, face_refs):
    for side, face_ref in zip((0, 1, 2 + odd[0], 3 - odd[0]), face_refs):
        for face in range(FACES):
            start = pl.multiple_of(face_rows[side, face] * BLOCK, BLOCK)
            upper = nodes_ref[pl.ds(start, 32), :]
            lower = nodes_ref[pl.ds(start + 32, 32), :]
            face_ref[face * 32 : (face + 1) * 32, :] = jnp.where(left_lanes(32), upper, lower)


def columns_of(step):
    return slice(step * STEP * BLOCK, (step + 1) * STEP * BLOCK)


def field_kernel(
    face_rows, odd, right_hbm, parts_ref, turned_ref, nodes_ref, out0, out1, out2, out3, right_ref, sems
):
    copies = []
    for step in range(GRID):
        columns = pl.ds(step * STEP * BLOCK, STEP * BLOCK)
        copies.append(
            pltpu.make_async_copy(right_hbm.at[:, columns], right_ref.at[step], sems.at[step])
        )
        copies[step].start()
    for step in range(GRID):
        copies[step].wait()
        lead, rest = halves_of(right_ref[step])
        columns = slice(step * STEP * BLOCK, (step + 1) * STEP * BLOCK)
        turned_ref[:RHS, columns] = lead
        turned_ref[RHS:, columns] = rest
        for chunk in range(STEP * BLOCK // LANES):
            piece = right_ref[step, :, chunk * LANES : (chunk + 1) * LANES]
            doubled = jnp.concatenate([piece, piece], axis=0).T
            start = step * STEP * BLOCK + chunk * LANES
            nodes_ref[start : start + LANES, :] = doubled
            halves = two_parts(doubled)
            parts_ref[step * STEP + 2 * chunk] = halves[:BLOCK]
            parts_ref[step * STEP + 2 * chunk + 1] = halves[BLOCK:]
    emit_faces(face_rows, odd, nodes_ref, (out0, out1, out2, out3))


def entries_kernel(raw_hbm, mats_ref, raw_ref, rows_ref, sems):
    half = left_lanes(32)
    lane = lax.broadcasted_iota(jnp.int32, (32, LANES), 1)
    twice = 2 * lax.broadcasted_iota(jnp.int32, (32, LANES), 0)
    shift_even = jnp.where(jnp.logical_and(half, lane == twice), SHIFT, 0.0)
    shift_odd = jnp.where(jnp.logical_and(half, lane == twice + 1), SHIFT, 0.0)

    def fetch(step):
        blocks = pl.ds(step * STEP, STEP)
        return pltpu.make_async_copy(raw_hbm.at[:, blocks], raw_ref.at[step], sems.at[step])

    for step in range(GRID):
        fetch(step).start()

    for step in range(GRID):
        fetch(step).wait()
        for k in range(COUPLED):
            for pair in range(32):
                rows_ref[pl.ds((k * 32 + pair) * STEP, STEP), :] = raw_ref[
                    step, k, :, pair * LANES : (pair + 1) * LANES
                ]
        for item in range(STEP):
            for duo in range(4):
                first = rows_ref[pl.ds(2 * duo * 256 + item, 32, stride=STEP), :]
                if 2 * duo + 1 < COUPLED:
                    second = rows_ref[pl.ds((2 * duo + 1) * 256 + item, 32, stride=STEP), :]
                else:
                    second = jnp.zeros_like(first)
                even = jnp.where(half, first, pltpu.roll(second, RHS, 1))
                odd = jnp.where(half, pltpu.roll(first, RHS, 1), second)
                if duo == 0:
                    even = even - shift_even
                    odd = odd - shift_odd
                lead, rest = halves_of(jnp.concatenate([even, odd], axis=0))
                block = step * STEP + item
                mats_ref[block, :BLOCK, duo * LANES : (duo + 1) * LANES] = lead
                mats_ref[block, BLOCK:, duo * LANES : (duo + 1) * LANES] = rest


def fill_extended(odd, parts_ref, received, extended_ref):
    extended_ref[:BLK_DEV] = parts_ref[...]
    half = left_lanes(32)
    for side, got_ref in zip((0, 1, 3 - odd[0], 2 + odd[0]), received):
        for face in range(FACES):
            packed = got_ref[face * 32 : (face + 1) * 32, :]
            turned = pltpu.roll(packed, RHS, 1)
            block = BLK_DEV + side * FACES + face
            extended_ref[block, :32] = two_parts(jnp.where(half, packed, turned))
            extended_ref[block, 32:] = two_parts(jnp.where(half, turned, packed))


def block_row(block, neighbours, mats_ref, extended_ref, nodes_ref):
    pieces = [extended_ref[block]]
    for k in range(COUPLED - 1):
        pieces.append(extended_ref[neighbours[k, block]])
    pieces.append(pieces[0])
    grid = product(mats_ref[block], jnp.concatenate(pieces, axis=0))
    folded = grid[:BLOCK] + grid[BLOCK:]
    doubled = folded + pltpu.roll(folded, RHS, 1)
    start = block * BLOCK
    nodes_ref[pl.ds(start, 32, stride=2), :] = doubled[:32]
    nodes_ref[pl.ds(start + 1, 32, stride=2), :] = doubled[32:]
    return nodes_ref[pl.ds(start, BLOCK), :]


def first_kernel(
    neighbours, face_rows, odd, mats_ref, parts_ref, own_ref, near, far, inner, outer,
    image_ref, both_ref, out0, out1, out2, out3, extended_ref, nodes_ref,
):
    fill_extended(odd, parts_ref, (near, far, inner, outer), extended_ref)
    for block in range(BLK_DEV):
        doubled = block_row(block, neighbours, mats_ref, extended_ref, nodes_ref)
        image_ref[block] = two_parts(doubled)
        rows = slice(block * BLOCK, (block + 1) * BLOCK)
        both_ref[rows, :] = jnp.where(left_lanes(BLOCK), own_ref[rows, :], doubled)
    emit_faces(face_rows, odd, nodes_ref, (out0, out1, out2, out3))


def quarter_sum(grid):
    tall = grid[:RHS] + grid[RHS:]
    return tall + pltpu.roll(tall, RHS, 1)


def rows_of(ref, step):
    return ref[step * STEP : (step + 1) * STEP].reshape(STEP * BLOCK, LANES)


def product(left, right):
    return jnp.dot(left, right, preferred_element_type=F32)


def gram_kernel(turned_ref, field_ref, image_ref, out_ref, image_turned_ref, wide_acc, acc_ref):
    wide_acc[...] = jnp.zeros_like(wide_acc)
    acc_ref[...] = jnp.zeros_like(acc_ref)
    for step in range(GRID):
        field = rows_of(field_ref, step)
        image = rows_of(image_ref, step)
        turned = image.T
        image_turned_ref[:, columns_of(step)] = turned
        wide_acc[...] += product(
            turned_ref[:, columns_of(step)], jnp.concatenate([field, image], axis=1)
        )
        acc_ref[...] += product(turned, image)
    out_ref[:RHS, :] = quarter_sum(wide_acc[:, :LANES])
    out_ref[RHS:LANES, :] = quarter_sum(wide_acc[:, LANES:])
    out_ref[LANES:, :] = quarter_sum(acc_ref[...])


def second_kernel(
    neighbours, odd, mats_ref, parts_ref, near, far, inner, outer, turned_ref, image_turned_ref,
    gram_ref, outgoing_ref, image_hbm, sums_ref, extended_ref, nodes_ref, image_ref, acc_ref, sem,
):
    fill_extended(odd, parts_ref, (near, far, inner, outer), extended_ref)
    acc_ref[...] = jnp.zeros_like(acc_ref)
    for block in range(BLK_DEV):
        doubled = block_row(block, neighbours, mats_ref, extended_ref, nodes_ref)
        image_ref[block] = two_parts(doubled)
    saving = pltpu.make_async_copy(image_ref, image_hbm, sem)
    saving.start()
    for step in range(GRID):
        columns = columns_of(step)
        both = jnp.concatenate([turned_ref[:, columns], image_turned_ref[:, columns]], axis=0)
        acc_ref[...] += product(both, rows_of(image_ref, step))
    pack_sums(
        gram_ref[:RHS, :],
        gram_ref[RHS:LANES, :],
        gram_ref[LANES:, :],
        quarter_sum(acc_ref[:LANES]),
        quarter_sum(acc_ref[LANES:]),
        sums_ref,
    )
    saving.wait()


def pack_sums(norm, curve, image_norm, far_field, far_image, sums_ref):
    half = left_lanes(RHS)
    row = lax.broadcasted_iota(jnp.int32, (RHS, LANES), 0)
    col = lax.broadcasted_iota(jnp.int32, (RHS, LANES), 1)
    col = jnp.where(half, col, col - RHS)
    upper = row <= col
    diagonal = jnp.sum(jnp.where(row == col, image_norm, 0.0), axis=0, keepdims=True)
    last = jnp.where(row == RHS - 2, diagonal[:, RHS - 1 : RHS], diagonal)
    square = far_image[:, :RHS]
    balanced = 0.5 * (square + square.T)
    balanced = jnp.concatenate([balanced, balanced], axis=1)
    packed = jnp.where(upper, balanced, last)
    sums_ref[:RHS, :] = jnp.where(half, jnp.where(upper, norm, image_norm), curve)
    sums_ref[RHS:, :] = jnp.where(half, far_field, packed)


def unpack_sums(sums_ref):
    pair = sums_ref[:RHS, :RHS]
    curve = sums_ref[:RHS, RHS:]
    far_field = sums_ref[RHS:, :RHS]
    packed = sums_ref[RHS:, RHS:]
    row = lax.broadcasted_iota(jnp.int32, (RHS, RHS), 0)
    col = lax.broadcasted_iota(jnp.int32, (RHS, RHS), 1)
    pair_t = pair.T
    packed_t = packed.T
    norm = jnp.where(row <= col, pair, pair_t)
    lanes = lax.broadcasted_iota(jnp.int32, (1, RHS), 1)
    diagonal = jnp.where(
        lanes == RHS - 1, packed[RHS - 2 : RHS - 1, :1], packed[RHS - 1 : RHS, :]
    )
    image_norm = jnp.where(row > col, pair, pair_t)
    image_norm = jnp.where(row == col, diagonal, image_norm)
    far_image = jnp.where(row <= col, packed, packed_t)
    return norm, curve, image_norm, far_field, far_image


def relay_kernel(owners, die_node, both_ref, out_ref, counts):
    out_ref[...] = jnp.zeros_like(out_ref)
    for owner in range(16):
        counts[owner] = owner * SLOTS

    def move(row, carry):
        owner = owners[row]
        slot = counts[owner]
        counts[owner] = slot + 1
        out_ref[pl.ds(slot, 1), :] = both_ref[pl.ds(die_node[row], 1), :]
        return carry

    lax.fori_loop(0, DIE_ROWS, move, 0, unroll=8)


def mul(left, right):
    return jnp.dot(left, right, precision=lax.Precision.HIGHEST, preferred_element_type=F32)


def mul_t(left, right):
    return lax.dot_general(
        left,
        right,
        (((1,), (1,)), ((), ())),
        precision=lax.Precision.HIGHEST,
        preferred_element_type=F32,
    )


def eliminate(systems):
    tall = 8
    spread = (tall, LANES)
    sub = lax.broadcasted_iota(jnp.int32, spread, 0)
    grids = [[system[tall * r : tall * r + tall] for r in range(RHS // tall)] for system in systems]
    for pivot in range(RHS // tall):
        base = tall * pivot
        for tiles in grids:
            rows = tiles[pivot]
            entry = {
                (i, j): jnp.broadcast_to(rows[i : i + 1, base + j : base + j + 1], spread)
                for i in range(tall)
                for j in range(i + 1)
            }
            inverse, lower = [], {}
            for r in range(tall):
                inverse.append(1.0 / entry[r, r])
                for i in range(r + 1, tall):
                    lower[i, r] = entry[i, r] * inverse[r]
                    for j in range(r + 1, i + 1):
                        entry[i, j] = entry[i, j] - lower[i, r] * entry[j, r]
            solved = [jnp.broadcast_to(rows[i : i + 1, :], spread) for i in range(tall)]
            for i in range(tall):
                for j in range(i):
                    solved[i] = solved[i] - lower[i, j] * solved[j]
            for i in reversed(range(tall)):
                solved[i] = solved[i] * inverse[i]
                for j in range(i + 1, tall):
                    solved[i] = solved[i] - lower[j, i] * solved[j]
            for r in range(RHS // tall):
                if r == pivot:
                    continue
                old = tiles[r]
                fresh = old
                for i in range(tall):
                    fresh = fresh - old[:, base + i : base + i + 1] * solved[i]
                tiles[r] = fresh
            merged = solved[0]
            for i in range(1, tall):
                merged = jnp.where(sub == i, solved[i], merged)
            tiles[pivot] = merged
    return [jnp.concatenate(tiles, axis=0)[:, RHS:] for tiles in grids]


def wide(left, right):
    return jnp.concatenate([left, right], axis=1)


def solve_steps(sums_ref):
    norm_zero, cross, image_norm, far_field, far_image = unpack_sums(sums_ref)
    eye = (
        lax.broadcasted_iota(jnp.int32, (RHS, RHS), 0)
        == lax.broadcasted_iota(jnp.int32, (RHS, RHS), 1)
    ).astype(F32)
    curve_zero = 0.5 * (cross + cross.T) + SHIFT * norm_zero
    alpha, norm_inverse = eliminate([wide(curve_zero, norm_zero), wide(norm_zero, eye)])
    alpha_t = alpha.T
    gram = jnp.concatenate([wide(norm_zero, cross), wide(cross.T, image_norm)], axis=0)
    shifted = jnp.concatenate([wide(cross, far_field), wide(image_norm, far_image)], axis=0)
    start = eye - SHIFT * alpha_t
    resid = wide(start, -alpha_t)
    norm_one = mul_t(mul(resid, gram), resid)
    mixed = start + mul(norm_inverse, norm_one).T
    direction = wide(mixed, -alpha_t)
    curve_one = mul_t(mul(direction, shifted + SHIFT * gram), direction)
    (alpha_two,) = eliminate([wide(0.5 * (curve_one + curve_one.T), norm_one)])
    second = mul(alpha_two.T, wide(mixed, alpha_t))
    gain, drop = second[:, :RHS], second[:, RHS:]
    keep = alpha_t + gain
    return keep, drop, start - SHIFT * gain, keep - SHIFT * drop


def halves_of(value):
    lead = value.astype(BF16)
    return lead, (value - lead.astype(F32)).astype(BF16)


def final_kernel(
    sums_ref, turned_ref, image_turned_ref, far_hbm, solution_hbm, residual_hbm, coef_ref,
    far_ref, solution_ref, residual_ref, far_sem, sems,
):
    fetch = pltpu.make_async_copy(far_hbm, far_ref, far_sem)
    fetch.start()
    keep, drop, left_over, taken = solve_steps(sums_ref)
    top = [wide(keep, keep), wide(-drop, -drop), jnp.zeros((RHS, LANES), F32)]
    low = [wide(left_over, left_over), wide(-taken, -taken), wide(drop, drop)]
    rows = jnp.concatenate(
        [jnp.concatenate(top, axis=1), jnp.concatenate(low, axis=1)], axis=0
    )
    weights = jnp.concatenate(halves_of(rows), axis=0)
    coef_ref[...] = jnp.concatenate([keep.T, -drop.T], axis=0)
    fetch.wait()
    copies = []
    for step in range(GRID):
        columns = columns_of(step)
        both = jnp.concatenate([turned_ref[:, columns], image_turned_ref[:, columns]], axis=0)
        mixed = product(weights[:, : 2 * LANES], both) + lax.dot_general(
            weights[:, 2 * LANES :],
            rows_of(far_ref, step),
            (((1,), (1,)), ((), ())),
            preferred_element_type=F32,
        )
        mixed = mixed[:LANES] + mixed[LANES:]
        solution_ref[:, columns] = mixed[:RHS]
        residual_ref[:, columns] = mixed[RHS:]
        part = pl.ds(step * STEP * BLOCK, STEP * BLOCK)
        for at, (source, target) in enumerate(
            ((solution_ref, solution_hbm), (residual_ref, residual_hbm))
        ):
            copies.append(
                pltpu.make_async_copy(source.at[:, part], target.at[:, part], sems.at[at, step])
            )
            copies[-1].start()
    for copy in copies:
        copy.wait()


def owner_kernel(coef_ref, got_ref, out_ref):
    coef = coef_ref[...]
    none = jnp.zeros_like(coef)
    square = jnp.concatenate([wide(coef, none), wide(none, coef)], axis=0)
    weights = jnp.concatenate(halves_of(square), axis=1)
    for pack in range(8):
        pieces = []
        for pair in range(8 * pack, 8 * pack + 8):
            pieces.append(
                wide(
                    got_ref[pl.ds(2 * pair, 16, stride=SLOTS), :],
                    got_ref[pl.ds(2 * pair + 1, 16, stride=SLOTS), :],
                )
            )
        rows = jnp.concatenate(pieces, axis=0)
        lead, rest = halves_of(rows)
        grid = product(jnp.concatenate([lead, rest], axis=0), weights)
        grid = grid[:LANES] + grid[LANES:]
        grid = grid[:, :LANES] + grid[:, LANES:]
        for at in range(8):
            pair = 8 * pack + at
            out_ref[:, pair * LANES : (pair + 1) * LANES] = grid[16 * at : 16 * at + 16]


def swap(shard, axis, bit):
    return lax.ppermute(shard, axis, [(i, i ^ bit) for i in range(lax.axis_size(axis))])


def exchange(faces):
    count = lax.axis_size("layer")
    top = lax.axis_size("region") // 2
    near = swap(faces[0], "region", 1)
    far = swap(faces[1], "region", top)
    inner = swap(faces[2], "layer", 1)
    pairs = [(i, i + 1) for i in range(1, count - 1, 2)]
    outer = lax.ppermute(faces[3], "layer", pairs + [(b, a) for a, b in pairs])
    return near, far, inner, outer


def total(local):
    layers = lax.axis_size("layer")
    regions = lax.axis_size("region")
    parts = local.reshape(layers, LANES // layers, LANES)
    mine = jnp.sum(lax.all_to_all(parts, "layer", 0, 0, tiled=True), axis=0)
    copies = jnp.broadcast_to(mine[None], (regions,) + mine.shape)
    mine = jnp.sum(lax.all_to_all(copies, "region", 0, 0, tiled=True), axis=0)
    copies = jnp.broadcast_to(mine[None], (layers,) + mine.shape)
    return lax.all_to_all(copies, "layer", 0, 0, tiled=True).reshape(LANES, LANES)


TURNED = jax.ShapeDtypeStruct((LANES, NODES_DEV), BF16)
PARTS = jax.ShapeDtypeStruct((BLK_DEV, BLOCK, LANES), BF16)
NODE_ROWS = jax.ShapeDtypeStruct((NODES_DEV, LANES), F32)
FACE = jax.ShapeDtypeStruct((FACES * 32, LANES), F32)
FIELD = jax.ShapeDtypeStruct((RHS, NODES_DEV), F32)


def on_device(right_side, block_entries, neighbours, face_rows, die_owner, die_node):
    owners = in_hbm(die_owner[:, 0])
    die_node = in_hbm(die_node)
    neighbours = in_hbm(neighbours.T)
    face_rows = in_hbm(face_rows)
    odd = (lax.axis_index("layer") % 2).astype(jnp.int32).reshape(1)
    entries = in_hbm(jnp.transpose(block_entries, (1, 0, 2)))
    right_side = in_hbm(right_side)
    outcome = pl.pallas_call(
        field_kernel,
        in_specs=[smem(), smem(), pl.BlockSpec(memory_space=pl.ANY)],
        out_specs=[resident()] * 7,
        out_shape=[PARTS, TURNED, NODE_ROWS] + [FACE] * 4,
        scratch_shapes=[
            pltpu.VMEM((GRID, RHS, STEP * BLOCK), F32),
            pltpu.SemaphoreType.DMA((GRID,)),
        ],
        compiler_params=params(8),
        cost_estimate=cost(1_000_000, 5_000_000),
        name="field",
    )(face_rows, odd, right_side)
    field, turned, own_rows, faces = outcome[0], outcome[1], outcome[2], outcome[3:]
    received = exchange(faces)
    mats = pl.pallas_call(
        entries_kernel,
        in_specs=[pl.BlockSpec(memory_space=pl.ANY)],
        out_specs=resident(),
        out_shape=jax.ShapeDtypeStruct((BLK_DEV, 2 * BLOCK, 4 * LANES), BF16),
        scratch_shapes=[
            pltpu.VMEM((GRID, COUPLED, STEP, BLOCK * BLOCK), F32),
            pltpu.VMEM((COUPLED * 32 * STEP, LANES), F32),
            pltpu.SemaphoreType.DMA((GRID,)),
        ],
        compiler_params=params(12),
        cost_estimate=cost(10_000_000, 16_000_000),
        name="entries",
    )(entries)
    apply_scratch = [
        pltpu.VMEM((BLK_DEV + 4 * FACES, BLOCK, LANES), BF16),
        pltpu.VMEM((NODES_DEV, LANES), F32),
    ]
    outcome = pl.pallas_call(
        first_kernel,
        in_specs=[smem(), smem(), smem()] + [resident()] * 7,
        out_specs=[resident()] * 6,
        out_shape=[PARTS, NODE_ROWS] + [FACE] * 4,
        scratch_shapes=apply_scratch,
        compiler_params=params(8),
        cost_estimate=cost(1_000_000_000, 16_000_000),
        name="first_image",
    )(neighbours, face_rows, odd, mats, field, own_rows, *received)
    image, both_rows, faces = outcome[0], outcome[1], outcome[2:]
    received = exchange(faces)
    grams, image_turned = pl.pallas_call(
        gram_kernel,
        in_specs=[resident()] * 3,
        out_specs=[resident()] * 2,
        out_shape=[jax.ShapeDtypeStruct((3 * RHS, LANES), F32), TURNED],
        scratch_shapes=[pltpu.VMEM((LANES, 2 * LANES), F32), pltpu.VMEM((LANES, LANES), F32)],
        compiler_params=params(8),
        cost_estimate=cost(500_000_000, 2_000_000),
        name="near_grams",
    )(turned, field, image)
    outgoing = pl.pallas_call(
        relay_kernel,
        in_specs=[smem(), smem(), resident()],
        out_specs=resident(),
        out_shape=jax.ShapeDtypeStruct((16 * SLOTS, LANES), F32),
        scratch_shapes=[pltpu.SMEM((16,), jnp.int32)],
        compiler_params=params(8),
        cost_estimate=cost(1_000_000, 10_000_000),
        name="relay_rows",
    )(owners, die_node, both_rows)
    relayed = lax.all_to_all(
        outgoing.reshape(16, SLOTS, LANES), "layer", 0, 0, tiled=True
    ).reshape(16 * SLOTS, LANES)
    far_image, local_sums = pl.pallas_call(
        second_kernel,
        in_specs=[smem(), smem()] + [resident()] * 9 + [pl.BlockSpec(memory_space=pl.ANY)],
        out_specs=[far_memory(), resident()],
        out_shape=[
            pltpu.HBM(PARTS.shape, BF16),
            jax.ShapeDtypeStruct((LANES, LANES), F32),
        ],
        scratch_shapes=apply_scratch
        + [
            pltpu.VMEM(PARTS.shape, BF16),
            pltpu.VMEM((2 * LANES, LANES), F32),
            pltpu.SemaphoreType.DMA,
        ],
        compiler_params=params(8),
        cost_estimate=cost(1_000_000_000, 14_000_000),
        name="second_image",
    )(neighbours, odd, mats, image, *received, turned, image_turned, grams, outgoing)
    sums = total(local_sums)
    solution_field, residual, coef = pl.pallas_call(
        final_kernel,
        in_specs=[resident()] * 3 + [far_memory()],
        out_specs=[far_memory()] * 2 + [resident()],
        out_shape=[FIELD, FIELD, jax.ShapeDtypeStruct((LANES, RHS), F32)],
        scratch_shapes=[
            pltpu.VMEM(PARTS.shape, BF16),
            pltpu.VMEM(FIELD.shape, F32),
            pltpu.VMEM(FIELD.shape, F32),
            pltpu.SemaphoreType.DMA,
            pltpu.SemaphoreType.DMA((2, GRID)),
        ],
        compiler_params=params(8),
        cost_estimate=cost(500_000_000, 8_000_000),
        name="final",
    )(sums, turned, image_turned, in_hbm(far_image))
    mech_temps = pl.pallas_call(
        owner_kernel,
        in_specs=[resident()] * 2,
        out_specs=resident(),
        out_shape=jax.ShapeDtypeStruct((16, SLOTS * RHS), F32),
        compiler_params=params(8),
        cost_estimate=cost(100_000_000, 2_000_000),
        name="owner_rows",
    )(coef, relayed)
    return solution_field, residual, mech_temps


def solution(mesh):
    in_specs = (
        P(None, ("region", "layer")),
        P(("region", "layer"), None, None),
        P(("region", "layer"), None),
        P(("region", "layer"), None),
        P(("region", "layer"), None),
        P(("region", "layer")),
    )
    out_specs = (
        P(None, ("region", "layer")),
        P(None, ("region", "layer")),
        P(("region", "layer"), None),
    )
    return jax.shard_map(
        on_device, mesh=mesh, in_specs=in_specs, out_specs=out_specs, check_vma=False
    )
```

```python
import functools

import jax
import jax.numpy as jnp
from jax import lax
from jax.experimental import pallas as pl
from jax.experimental.pallas import tpu as pltpu
from jax.sharding import PartitionSpec as P

BLOCK = 64
RHS = 64
COUPLED = 7
BLK_DEV = 64
NODES_DEV = BLK_DEV * BLOCK
DIE_ROWS = 512
SLOTS = 128
FACES = 8
LANES = 128
STEP = 8
GRID = BLK_DEV // STEP
SHIFT = 1.5
BF16 = jnp.bfloat16
F32 = jnp.float32


def params(mib):
    return pltpu.CompilerParams(vmem_limit_bytes=mib * 1024 * 1024)


def far_memory():
    return pl.BlockSpec(memory_space=pltpu.HBM)


def in_hbm(array):
    return pltpu.with_memory_space_constraint(array, pltpu.HBM)


def cost(flops, moved):
    return pl.CostEstimate(flops=flops, bytes_accessed=moved, transcendentals=0)


def resident():
    return pl.BlockSpec(memory_space=pltpu.VMEM)


def fetch_tables(sources, targets, sems):
    copies = [
        pltpu.make_async_copy(source, target, sems.at[at])
        for at, (source, target) in enumerate(zip(sources, targets))
    ]
    for copy in copies:
        copy.start()
    return copies


def tables(*shapes):
    return [pltpu.SMEM(shape, jnp.int32) for shape in shapes] + [
        pltpu.SemaphoreType.DMA((len(shapes),))
    ]


def left_lanes(rows):
    return lax.broadcasted_iota(jnp.int32, (rows, LANES), 1) < RHS


def two_parts(doubled):
    lead = doubled.astype(BF16).astype(F32)
    return jnp.where(left_lanes(doubled.shape[0]), lead, doubled - lead).astype(BF16)


def emit_faces(face_rows, odd, nodes_ref, face_refs):
    for side, face_ref in zip((0, 1, 2 + odd[0], 3 - odd[0]), face_refs):
        for face in range(FACES):
            start = pl.multiple_of(face_rows[side, face] * BLOCK, BLOCK)
            upper = nodes_ref[pl.ds(start, 32), :]
            lower = nodes_ref[pl.ds(start + 32, 32), :]
            face_ref[face * 32 : (face + 1) * 32, :] = jnp.where(left_lanes(32), upper, lower)


def columns_of(step):
    return slice(step * STEP * BLOCK, (step + 1) * STEP * BLOCK)


def field_kernel(
    face_hbm, odd_hbm, right_hbm, right_ref, nodes_ref, out0, out1, out2, out3, sems,
    face_rows, odd, table_sems,
):
    waits = fetch_tables((face_hbm, odd_hbm), (face_rows, odd), table_sems)
    copies = []
    for step in range(GRID):
        columns = pl.ds(step * STEP * BLOCK, STEP * BLOCK)
        copies.append(
            pltpu.make_async_copy(
                right_hbm.at[:, columns], right_ref.at[:, columns], sems.at[step]
            )
        )
        copies[step].start()
    for step in range(GRID):
        copies[step].wait()
        for chunk in range(STEP * BLOCK // LANES):
            start = step * STEP * BLOCK + chunk * LANES
            piece = right_ref[:, start : start + LANES]
            nodes_ref[start : start + LANES, :] = jnp.concatenate([piece, piece], axis=0).T
    for wait in waits:
        wait.wait()
    emit_faces(face_rows, odd, nodes_ref, (out0, out1, out2, out3))


def entries_kernel(
    raw_hbm, right_ref, nodes_ref, mats_ref, parts_ref, turned_ref, raw_ref, rows_ref, sems
):
    half = left_lanes(32)
    lane = lax.broadcasted_iota(jnp.int32, (32, LANES), 1)
    twice = 2 * lax.broadcasted_iota(jnp.int32, (32, LANES), 0)
    shift_even = jnp.where(jnp.logical_and(half, lane == twice), SHIFT, 0.0)
    shift_odd = jnp.where(jnp.logical_and(half, lane == twice + 1), SHIFT, 0.0)

    def fetch(step):
        blocks = pl.ds(step * STEP, STEP)
        return pltpu.make_async_copy(raw_hbm.at[:, blocks], raw_ref.at[step], sems.at[step])

    for step in range(GRID):
        fetch(step).start()
    for step in range(GRID):
        columns = columns_of(step)
        lead, rest = halves_of(right_ref[:, columns])
        turned_ref[:RHS, columns] = lead
        turned_ref[RHS:, columns] = rest
    for block in range(BLK_DEV):
        parts_ref[block] = two_parts(nodes_ref[block * BLOCK : (block + 1) * BLOCK, :])
    for step in range(GRID):
        fetch(step).wait()
        for k in range(COUPLED):
            for pair in range(32):
                rows_ref[pl.ds((k * 32 + pair) * STEP, STEP), :] = raw_ref[
                    step, k, :, pair * LANES : (pair + 1) * LANES
                ]
        for item in range(STEP):
            for duo in range(4):
                first = rows_ref[pl.ds(2 * duo * 256 + item, 32, stride=STEP), :]
                if 2 * duo + 1 < COUPLED:
                    second = rows_ref[pl.ds((2 * duo + 1) * 256 + item, 32, stride=STEP), :]
                else:
                    second = jnp.zeros_like(first)
                even = jnp.where(half, first, pltpu.roll(second, RHS, 1))
                odd = jnp.where(half, pltpu.roll(first, RHS, 1), second)
                if duo == 0:
                    even = even - shift_even
                    odd = odd - shift_odd
                lead, rest = halves_of(jnp.concatenate([even, odd], axis=0))
                block = step * STEP + item
                mats_ref[block, :BLOCK, duo * LANES : (duo + 1) * LANES] = lead
                mats_ref[block, BLOCK:, duo * LANES : (duo + 1) * LANES] = rest


def own_extended(parts_ref, extended_ref):
    extended_ref[:BLK_DEV] = parts_ref[...]


def fill_extended(odd, received, extended_ref):
    half = left_lanes(32)
    for side, got_ref in zip((0, 1, 3 - odd[0], 2 + odd[0]), received):
        for face in range(FACES):
            packed = got_ref[face * 32 : (face + 1) * 32, :]
            turned = pltpu.roll(packed, RHS, 1)
            block = BLK_DEV + side * FACES + face
            extended_ref[block, :32] = two_parts(jnp.where(half, packed, turned))
            extended_ref[block, 32:] = two_parts(jnp.where(half, turned, packed))


def block_row(block, neighbours, mats_ref, extended_ref, nodes_ref):
    pieces = [extended_ref[block]]
    for k in range(COUPLED - 1):
        pieces.append(extended_ref[neighbours[k, block]])
    pieces.append(pieces[0])
    grid = product(mats_ref[block], jnp.concatenate(pieces, axis=0))
    folded = grid[:BLOCK] + grid[BLOCK:]
    doubled = folded + pltpu.roll(folded, RHS, 1)
    start = block * BLOCK
    nodes_ref[pl.ds(start, 32, stride=2), :] = doubled[:32]
    nodes_ref[pl.ds(start + 1, 32, stride=2), :] = doubled[32:]
    return nodes_ref[pl.ds(start, BLOCK), :]


def first_kernel(
    neighbours_hbm, face_hbm, odd_hbm, mats_ref, parts_ref, own_ref, near, far, inner, outer,
    image_ref, both_ref, out0, out1, out2, out3, extended_ref, nodes_ref,
    neighbours, face_rows, odd, table_sems,
):
    waits = fetch_tables(
        (neighbours_hbm, face_hbm, odd_hbm), (neighbours, face_rows, odd), table_sems
    )
    own_extended(parts_ref, extended_ref)
    for wait in waits:
        wait.wait()
    fill_extended(odd, (near, far, inner, outer), extended_ref)
    for block in range(BLK_DEV):
        doubled = block_row(block, neighbours, mats_ref, extended_ref, nodes_ref)
        image_ref[block] = two_parts(doubled)
        rows = slice(block * BLOCK, (block + 1) * BLOCK)
        both_ref[rows, :] = jnp.where(left_lanes(BLOCK), own_ref[rows, :], doubled)
    emit_faces(face_rows, odd, nodes_ref, (out0, out1, out2, out3))


def quarter_sum(grid):
    tall = grid[:RHS] + grid[RHS:]
    return tall + pltpu.roll(tall, RHS, 1)


def rows_of(ref, step):
    return ref[step * STEP : (step + 1) * STEP].reshape(STEP * BLOCK, LANES)


def product(left, right):
    return jnp.dot(left, right, preferred_element_type=F32)


def gram_kernel(turned_ref, field_ref, image_ref, out_ref, image_turned_ref, wide_acc, acc_ref):
    wide_acc[...] = jnp.zeros_like(wide_acc)
    acc_ref[...] = jnp.zeros_like(acc_ref)
    for step in range(GRID):
        field = rows_of(field_ref, step)
        image = rows_of(image_ref, step)
        turned = image.T
        image_turned_ref[:, columns_of(step)] = turned
        wide_acc[...] += product(
            turned_ref[:, columns_of(step)], jnp.concatenate([field, image], axis=1)
        )
        acc_ref[...] += product(turned, image)
    out_ref[:RHS, :] = quarter_sum(wide_acc[:, :LANES])
    out_ref[RHS:LANES, :] = quarter_sum(wide_acc[:, LANES:])
    out_ref[LANES:, :] = quarter_sum(acc_ref[...])


def second_kernel(
    neighbours_hbm, odd_hbm, mats_ref, parts_ref, near, far, inner, outer, turned_ref, image_turned_ref,
    gram_ref, outgoing_ref, image_hbm, sums_ref, extended_ref, nodes_ref, image_ref, acc_ref, sem,
    neighbours, odd, table_sems,
):
    waits = fetch_tables((neighbours_hbm, odd_hbm), (neighbours, odd), table_sems)
    own_extended(parts_ref, extended_ref)
    for wait in waits:
        wait.wait()
    fill_extended(odd, (near, far, inner, outer), extended_ref)
    acc_ref[...] = jnp.zeros_like(acc_ref)
    for block in range(BLK_DEV):
        doubled = block_row(block, neighbours, mats_ref, extended_ref, nodes_ref)
        image_ref[block] = two_parts(doubled)
    saving = pltpu.make_async_copy(image_ref, image_hbm, sem)
    saving.start()
    for step in range(GRID):
        columns = columns_of(step)
        both = jnp.concatenate([turned_ref[:, columns], image_turned_ref[:, columns]], axis=0)
        acc_ref[...] += product(both, rows_of(image_ref, step))
    pack_sums(
        gram_ref[:RHS, :],
        gram_ref[RHS:LANES, :],
        gram_ref[LANES:, :],
        quarter_sum(acc_ref[:LANES]),
        quarter_sum(acc_ref[LANES:]),
        sums_ref,
    )
    saving.wait()


def pack_sums(norm, curve, image_norm, far_field, far_image, sums_ref):
    half = left_lanes(RHS)
    row = lax.broadcasted_iota(jnp.int32, (RHS, LANES), 0)
    col = lax.broadcasted_iota(jnp.int32, (RHS, LANES), 1)
    col = jnp.where(half, col, col - RHS)
    upper = row <= col
    diagonal = jnp.sum(jnp.where(row == col, image_norm, 0.0), axis=0, keepdims=True)
    last = jnp.where(row == RHS - 2, diagonal[:, RHS - 1 : RHS], diagonal)
    square = far_image[:, :RHS]
    balanced = 0.5 * (square + square.T)
    balanced = jnp.concatenate([balanced, balanced], axis=1)
    packed = jnp.where(upper, balanced, last)
    sums_ref[:RHS, :] = jnp.where(half, jnp.where(upper, norm, image_norm), curve)
    sums_ref[RHS:, :] = jnp.where(half, far_field, packed)


def unpack_sums(sums_ref):
    pair = sums_ref[:RHS, :RHS]
    curve = sums_ref[:RHS, RHS:]
    far_field = sums_ref[RHS:, :RHS]
    packed = sums_ref[RHS:, RHS:]
    row = lax.broadcasted_iota(jnp.int32, (RHS, RHS), 0)
    col = lax.broadcasted_iota(jnp.int32, (RHS, RHS), 1)
    pair_t = pair.T
    packed_t = packed.T
    norm = jnp.where(row <= col, pair, pair_t)
    lanes = lax.broadcasted_iota(jnp.int32, (1, RHS), 1)
    diagonal = jnp.where(
        lanes == RHS - 1, packed[RHS - 2 : RHS - 1, :1], packed[RHS - 1 : RHS, :]
    )
    image_norm = jnp.where(row > col, pair, pair_t)
    image_norm = jnp.where(row == col, diagonal, image_norm)
    far_image = jnp.where(row <= col, packed, packed_t)
    return norm, curve, image_norm, far_field, far_image


def relay_kernel(
    owners_hbm, node_hbm, both_ref, out_ref, counts, owners, die_node, table_sems
):
    waits = fetch_tables((owners_hbm, node_hbm), (owners, die_node), table_sems)
    out_ref[...] = jnp.zeros_like(out_ref)
    for owner in range(16):
        counts[owner] = owner * SLOTS
    for wait in waits:
        wait.wait()

    def move(row, carry):
        owner = owners[row]
        slot = counts[owner]
        counts[owner] = slot + 1
        out_ref[pl.ds(slot, 1), :] = both_ref[pl.ds(die_node[row], 1), :]
        return carry

    lax.fori_loop(0, DIE_ROWS, move, 0, unroll=8)


def mul(left, right):
    return jnp.dot(left, right, precision=lax.Precision.HIGHEST, preferred_element_type=F32)


def mul_t(left, right):
    return lax.dot_general(
        left,
        right,
        (((1,), (1,)), ((), ())),
        precision=lax.Precision.HIGHEST,
        preferred_element_type=F32,
    )


def eliminate(systems):
    tall = 8
    spread = (tall, LANES)
    sub = lax.broadcasted_iota(jnp.int32, spread, 0)
    grids = [[system[tall * r : tall * r + tall] for r in range(RHS // tall)] for system in systems]
    for pivot in range(RHS // tall):
        base = tall * pivot
        for tiles in grids:
            rows = tiles[pivot]
            entry = {
                (i, j): jnp.broadcast_to(rows[i : i + 1, base + j : base + j + 1], spread)
                for i in range(tall)
                for j in range(i + 1)
            }
            inverse, lower = [], {}
            for r in range(tall):
                inverse.append(1.0 / entry[r, r])
                for i in range(r + 1, tall):
                    lower[i, r] = entry[i, r] * inverse[r]
                    for j in range(r + 1, i + 1):
                        entry[i, j] = entry[i, j] - lower[i, r] * entry[j, r]
            solved = [jnp.broadcast_to(rows[i : i + 1, :], spread) for i in range(tall)]
            for i in range(tall):
                for j in range(i):
                    solved[i] = solved[i] - lower[i, j] * solved[j]
            for i in reversed(range(tall)):
                solved[i] = solved[i] * inverse[i]
                for j in range(i + 1, tall):
                    solved[i] = solved[i] - lower[j, i] * solved[j]
            for r in range(RHS // tall):
                if r == pivot:
                    continue
                old = tiles[r]
                fresh = old
                for i in range(tall):
                    fresh = fresh - old[:, base + i : base + i + 1] * solved[i]
                tiles[r] = fresh
            merged = solved[0]
            for i in range(1, tall):
                merged = jnp.where(sub == i, solved[i], merged)
            tiles[pivot] = merged
    return [jnp.concatenate(tiles, axis=0)[:, RHS:] for tiles in grids]


def wide(left, right):
    return jnp.concatenate([left, right], axis=1)


def solve_steps(sums_ref):
    norm_zero, cross, image_norm, far_field, far_image = unpack_sums(sums_ref)
    eye = (
        lax.broadcasted_iota(jnp.int32, (RHS, RHS), 0)
        == lax.broadcasted_iota(jnp.int32, (RHS, RHS), 1)
    ).astype(F32)
    curve_zero = 0.5 * (cross + cross.T) + SHIFT * norm_zero
    alpha, norm_inverse = eliminate([wide(curve_zero, norm_zero), wide(norm_zero, eye)])
    alpha_t = alpha.T
    gram = jnp.concatenate([wide(norm_zero, cross), wide(cross.T, image_norm)], axis=0)
    shifted = jnp.concatenate([wide(cross, far_field), wide(image_norm, far_image)], axis=0)
    start = eye - SHIFT * alpha_t
    resid = wide(start, -alpha_t)
    norm_one = mul_t(mul(resid, gram), resid)
    mixed = start + mul(norm_inverse, norm_one).T
    direction = wide(mixed, -alpha_t)
    curve_one = mul_t(mul(direction, shifted + SHIFT * gram), direction)
    (alpha_two,) = eliminate([wide(0.5 * (curve_one + curve_one.T), norm_one)])
    second = mul(alpha_two.T, wide(mixed, alpha_t))
    gain, drop = second[:, :RHS], second[:, RHS:]
    keep = alpha_t + gain
    return keep, drop, start - SHIFT * gain, keep - SHIFT * drop


def halves_of(value):
    lead = value.astype(BF16)
    return lead, (value - lead.astype(F32)).astype(BF16)


def final_kernel(
    sums_ref, turned_ref, image_turned_ref, far_hbm, solution_hbm, residual_hbm, coef_ref,
    far_ref, solution_ref, residual_ref, far_sem, sems,
):
    fetch = pltpu.make_async_copy(far_hbm, far_ref, far_sem)
    fetch.start()
    keep, drop, left_over, taken = solve_steps(sums_ref)
    top = [wide(keep, keep), wide(-drop, -drop), jnp.zeros((RHS, LANES), F32)]
    low = [wide(left_over, left_over), wide(-taken, -taken), wide(drop, drop)]
    rows = jnp.concatenate(
        [jnp.concatenate(top, axis=1), jnp.concatenate(low, axis=1)], axis=0
    )
    weights = jnp.concatenate(halves_of(rows), axis=0)
    coef_ref[...] = jnp.concatenate([keep.T, -drop.T], axis=0)
    fetch.wait()
    copies = []
    for step in range(GRID):
        columns = columns_of(step)
        both = jnp.concatenate([turned_ref[:, columns], image_turned_ref[:, columns]], axis=0)
        mixed = product(weights[:, : 2 * LANES], both) + lax.dot_general(
            weights[:, 2 * LANES :],
            rows_of(far_ref, step),
            (((1,), (1,)), ((), ())),
            preferred_element_type=F32,
        )
        mixed = mixed[:LANES] + mixed[LANES:]
        solution_ref[:, columns] = mixed[:RHS]
        residual_ref[:, columns] = mixed[RHS:]
        part = pl.ds(step * STEP * BLOCK, STEP * BLOCK)
        for at, (source, target) in enumerate(
            ((solution_ref, solution_hbm), (residual_ref, residual_hbm))
        ):
            copies.append(
                pltpu.make_async_copy(source.at[:, part], target.at[:, part], sems.at[at, step])
            )
            copies[-1].start()
    for copy in copies:
        copy.wait()


def owner_kernel(coef_ref, got_ref, out_hbm, out_ref, sems):
    coef = coef_ref[...]
    none = jnp.zeros_like(coef)
    square = jnp.concatenate([wide(coef, none), wide(none, coef)], axis=0)
    weights = jnp.concatenate(halves_of(square), axis=1)

    def save(at):
        part = pl.ds(at * 32 * LANES, 32 * LANES)
        return pltpu.make_async_copy(out_ref.at[:, part], out_hbm.at[:, part], sems.at[at])

    for pack in range(8):
        pieces = []
        for pair in range(8 * pack, 8 * pack + 8):
            pieces.append(
                wide(
                    got_ref[pl.ds(2 * pair, 16, stride=SLOTS), :],
                    got_ref[pl.ds(2 * pair + 1, 16, stride=SLOTS), :],
                )
            )
        rows = jnp.concatenate(pieces, axis=0)
        lead, rest = halves_of(rows)
        grid = product(jnp.concatenate([lead, rest], axis=0), weights)
        grid = grid[:LANES] + grid[LANES:]
        grid = grid[:, :LANES] + grid[:, LANES:]
        for at in range(8):
            pair = 8 * pack + at
            out_ref[:, pair * LANES : (pair + 1) * LANES] = grid[16 * at : 16 * at + 16]
        if pack % 4 == 3:
            save(pack // 4).start()
    for at in range(2):
        save(at).wait()


def swap(shard, axis, bit):
    return lax.ppermute(shard, axis, [(i, i ^ bit) for i in range(lax.axis_size(axis))])


def exchange(faces):
    count = lax.axis_size("layer")
    top = lax.axis_size("region") // 2
    near = swap(faces[0], "region", 1)
    far = swap(faces[1], "region", top)
    inner = swap(faces[2], "layer", 1)
    pairs = [(i, i + 1) for i in range(1, count - 1, 2)]
    outer = lax.ppermute(faces[3], "layer", pairs + [(b, a) for a, b in pairs])
    return near, far, inner, outer


def total(local):
    layers = lax.axis_size("layer")
    regions = lax.axis_size("region")
    parts = local.reshape(layers, LANES // layers, LANES)
    mine = jnp.sum(lax.all_to_all(parts, "layer", 0, 0, tiled=True), axis=0)
    copies = jnp.broadcast_to(mine[None], (regions,) + mine.shape)
    mine = jnp.sum(lax.all_to_all(copies, "region", 0, 0, tiled=True), axis=0)
    copies = jnp.broadcast_to(mine[None], (layers,) + mine.shape)
    return lax.all_to_all(copies, "layer", 0, 0, tiled=True).reshape(LANES, LANES)


TURNED = jax.ShapeDtypeStruct((LANES, NODES_DEV), BF16)
PARTS = jax.ShapeDtypeStruct((BLK_DEV, BLOCK, LANES), BF16)
NODE_ROWS = jax.ShapeDtypeStruct((NODES_DEV, LANES), F32)
FACE = jax.ShapeDtypeStruct((FACES * 32, LANES), F32)
FIELD = jax.ShapeDtypeStruct((RHS, NODES_DEV), F32)


def on_device(right_side, block_entries, neighbours, face_rows, die_owner, die_node):
    owners = in_hbm(die_owner[:, 0])
    die_node = in_hbm(die_node)
    neighbours = in_hbm(neighbours.T)
    face_rows = in_hbm(face_rows)
    odd = (lax.axis_index("layer") % 2).astype(jnp.int32).reshape(1)
    entries = in_hbm(jnp.transpose(block_entries, (1, 0, 2)))
    right_side = in_hbm(right_side)
    outcome = pl.pallas_call(
        field_kernel,
        in_specs=[pl.BlockSpec(memory_space=pl.ANY)] * 3,
        out_specs=[resident()] * 6,
        out_shape=[FIELD, NODE_ROWS] + [FACE] * 4,
        scratch_shapes=[pltpu.SemaphoreType.DMA((GRID,))] + tables((4, FACES), (1,)),
        compiler_params=params(8),
        cost_estimate=cost(1_000_000, 5_000_000),
        name="field",
    )(face_rows, odd, right_side)
    right_rows, own_rows, faces = outcome[0], outcome[1], outcome[2:]
    received = exchange(faces)
    mats, field, turned = pl.pallas_call(
        entries_kernel,
        in_specs=[pl.BlockSpec(memory_space=pl.ANY)] + [resident()] * 2,
        out_specs=[resident()] * 3,
        out_shape=[
            jax.ShapeDtypeStruct((BLK_DEV, 2 * BLOCK, 4 * LANES), BF16),
            PARTS,
            TURNED,
        ],
        scratch_shapes=[
            pltpu.VMEM((GRID, COUPLED, STEP, BLOCK * BLOCK), F32),
            pltpu.VMEM((COUPLED * 32 * STEP, LANES), F32),
            pltpu.SemaphoreType.DMA((GRID,)),
        ],
        compiler_params=params(12),
        cost_estimate=cost(10_000_000, 16_000_000),
        name="entries",
    )(entries, right_rows, own_rows)
    apply_scratch = [
        pltpu.VMEM((BLK_DEV + 4 * FACES, BLOCK, LANES), BF16),
        pltpu.VMEM((NODES_DEV, LANES), F32),
    ]
    outcome = pl.pallas_call(
        first_kernel,
        in_specs=[pl.BlockSpec(memory_space=pl.ANY)] * 3 + [resident()] * 7,
        out_specs=[resident()] * 6,
        out_shape=[PARTS, NODE_ROWS] + [FACE] * 4,
        scratch_shapes=apply_scratch + tables((COUPLED - 1, BLK_DEV), (4, FACES), (1,)),
        compiler_params=params(8),
        cost_estimate=cost(1_000_000_000, 16_000_000),
        name="first_image",
    )(neighbours, face_rows, odd, mats, field, own_rows, *received)
    image, both_rows, faces = outcome[0], outcome[1], outcome[2:]
    received = exchange(faces)
    grams, image_turned = pl.pallas_call(
        gram_kernel,
        in_specs=[resident()] * 3,
        out_specs=[resident()] * 2,
        out_shape=[jax.ShapeDtypeStruct((3 * RHS, LANES), F32), TURNED],
        scratch_shapes=[pltpu.VMEM((LANES, 2 * LANES), F32), pltpu.VMEM((LANES, LANES), F32)],
        compiler_params=params(8),
        cost_estimate=cost(500_000_000, 2_000_000),
        name="near_grams",
    )(turned, field, image)
    outgoing = pl.pallas_call(
        relay_kernel,
        in_specs=[pl.BlockSpec(memory_space=pl.ANY)] * 2 + [resident()],
        out_specs=resident(),
        out_shape=jax.ShapeDtypeStruct((16 * SLOTS, LANES), F32),
        scratch_shapes=[pltpu.SMEM((16,), jnp.int32)] + tables((DIE_ROWS,), (DIE_ROWS,)),
        compiler_params=params(8),
        cost_estimate=cost(1_000_000, 10_000_000),
        name="relay_rows",
    )(owners, die_node, both_rows)
    relayed = lax.all_to_all(
        outgoing.reshape(16, SLOTS, LANES), "layer", 0, 0, tiled=True
    ).reshape(16 * SLOTS, LANES)
    far_image, local_sums = pl.pallas_call(
        second_kernel,
        in_specs=[pl.BlockSpec(memory_space=pl.ANY)] * 2
        + [resident()] * 9
        + [pl.BlockSpec(memory_space=pl.ANY)],
        out_specs=[far_memory(), resident()],
        out_shape=[
            pltpu.HBM(PARTS.shape, BF16),
            jax.ShapeDtypeStruct((LANES, LANES), F32),
        ],
        scratch_shapes=apply_scratch
        + [
            pltpu.VMEM(PARTS.shape, BF16),
            pltpu.VMEM((2 * LANES, LANES), F32),
            pltpu.SemaphoreType.DMA,
        ]
        + tables((COUPLED - 1, BLK_DEV), (1,)),
        compiler_params=params(8),
        cost_estimate=cost(1_000_000_000, 14_000_000),
        name="second_image",
    )(neighbours, odd, mats, image, *received, turned, image_turned, grams, outgoing)
    sums = total(local_sums)
    solution_field, residual, coef = pl.pallas_call(
        final_kernel,
        in_specs=[resident()] * 3 + [far_memory()],
        out_specs=[far_memory()] * 2 + [resident()],
        out_shape=[FIELD, FIELD, jax.ShapeDtypeStruct((LANES, RHS), F32)],
        scratch_shapes=[
            pltpu.VMEM(PARTS.shape, BF16),
            pltpu.VMEM(FIELD.shape, F32),
            pltpu.VMEM(FIELD.shape, F32),
            pltpu.SemaphoreType.DMA,
            pltpu.SemaphoreType.DMA((2, GRID)),
        ],
        compiler_params=params(8),
        cost_estimate=cost(500_000_000, 8_000_000),
        name="final",
    )(sums, turned, image_turned, in_hbm(far_image))
    mech_temps = pl.pallas_call(
        owner_kernel,
        in_specs=[resident()] * 2,
        out_specs=far_memory(),
        out_shape=jax.ShapeDtypeStruct((16, SLOTS * RHS), F32),
        scratch_shapes=[
            pltpu.VMEM((16, SLOTS * RHS), F32),
            pltpu.SemaphoreType.DMA((2,)),
        ],
        compiler_params=params(8),
        cost_estimate=cost(100_000_000, 2_000_000),
        name="owner_rows",
    )(coef, relayed)
    return solution_field, residual, mech_temps


def solution(mesh):
    in_specs = (
        P(None, ("region", "layer")),
        P(("region", "layer"), None, None),
        P(("region", "layer"), None),
        P(("region", "layer"), None),
        P(("region", "layer"), None),
        P(("region", "layer")),
    )
    out_specs = (
        P(None, ("region", "layer")),
        P(None, ("region", "layer")),
        P(("region", "layer"), None),
    )
    return jax.shard_map(
        on_device, mesh=mesh, in_specs=in_specs, out_specs=out_specs, check_vma=False
    )
```

```python
import functools

import jax
import jax.numpy as jnp
from jax import lax
from jax.experimental import pallas as pl
from jax.experimental.pallas import tpu as pltpu
from jax.sharding import PartitionSpec as P

BLOCK = 64
RHS = 64
COUPLED = 7
BLK_DEV = 64
NODES_DEV = BLK_DEV * BLOCK
DIE_ROWS = 512
SLOTS = 128
FACES = 8
LANES = 128
STEP = 8
GRID = BLK_DEV // STEP
SHIFT = 1.5
BF16 = jnp.bfloat16
F32 = jnp.float32


def params(mib):
    return pltpu.CompilerParams(vmem_limit_bytes=mib * 1024 * 1024)


def far_memory():
    return pl.BlockSpec(memory_space=pltpu.HBM)


def in_hbm(array):
    return pltpu.with_memory_space_constraint(array, pltpu.HBM)


def cost(flops, moved):
    return pl.CostEstimate(flops=flops, bytes_accessed=moved, transcendentals=0)


def resident():
    return pl.BlockSpec(memory_space=pltpu.VMEM)


def fetch_tables(sources, targets, sems):
    copies = [
        pltpu.make_async_copy(source, target, sems.at[at])
        for at, (source, target) in enumerate(zip(sources, targets))
    ]
    for copy in copies:
        copy.start()
    return copies


def tables(*shapes):
    return [pltpu.SMEM(shape, jnp.int32) for shape in shapes] + [
        pltpu.SemaphoreType.DMA((len(shapes),))
    ]


def left_lanes(rows):
    return lax.broadcasted_iota(jnp.int32, (rows, LANES), 1) < RHS


def two_parts(doubled):
    lead = doubled.astype(BF16).astype(F32)
    return jnp.where(left_lanes(doubled.shape[0]), lead, doubled - lead).astype(BF16)


def emit_faces(face_rows, odd, nodes_ref, face_refs):
    for side, face_ref in zip((1, 0, 2 + odd[0], 3 - odd[0]), face_refs):
        for face in range(FACES):
            start = pl.multiple_of(face_rows[side, face] * BLOCK, BLOCK)
            upper = nodes_ref[pl.ds(start, 32), :]
            lower = nodes_ref[pl.ds(start + 32, 32), :]
            face_ref[face * 32 : (face + 1) * 32, :] = jnp.where(left_lanes(32), upper, lower)


def columns_of(step):
    return slice(step * STEP * BLOCK, (step + 1) * STEP * BLOCK)


def field_kernel(
    face_hbm, odd_hbm, right_hbm, right_ref, nodes_ref, out0, out1, out2, out3, sems,
    face_rows, odd, table_sems,
):
    waits = fetch_tables((face_hbm, odd_hbm), (face_rows, odd), table_sems)
    copies = []
    for step in range(GRID):
        columns = pl.ds(step * STEP * BLOCK, STEP * BLOCK)
        copies.append(
            pltpu.make_async_copy(
                right_hbm.at[:, columns], right_ref.at[:, columns], sems.at[step]
            )
        )
        copies[step].start()
    for step in range(GRID):
        copies[step].wait()
        for chunk in range(STEP * BLOCK // LANES):
            start = step * STEP * BLOCK + chunk * LANES
            piece = right_ref[:, start : start + LANES]
            nodes_ref[start : start + LANES, :] = jnp.concatenate([piece, piece], axis=0).T
    for wait in waits:
        wait.wait()
    emit_faces(face_rows, odd, nodes_ref, (out0, out1, out2, out3))


def entries_kernel(
    raw_hbm, right_ref, nodes_ref, mats_ref, parts_ref, turned_ref, raw_ref, rows_ref, sems
):
    half = left_lanes(32)
    lane = lax.broadcasted_iota(jnp.int32, (32, LANES), 1)
    twice = 2 * lax.broadcasted_iota(jnp.int32, (32, LANES), 0)
    shift_even = jnp.where(jnp.logical_and(half, lane == twice), SHIFT, 0.0)
    shift_odd = jnp.where(jnp.logical_and(half, lane == twice + 1), SHIFT, 0.0)

    def fetch(step):
        blocks = pl.ds(step * STEP, STEP)
        return pltpu.make_async_copy(raw_hbm.at[:, blocks], raw_ref.at[step], sems.at[step])

    for step in range(GRID):
        fetch(step).start()
    for step in range(GRID):
        columns = columns_of(step)
        lead, rest = halves_of(right_ref[:, columns])
        turned_ref[:RHS, columns] = lead
        turned_ref[RHS:, columns] = rest
    for block in range(BLK_DEV):
        parts_ref[block] = two_parts(nodes_ref[block * BLOCK : (block + 1) * BLOCK, :])
    for step in range(GRID):
        fetch(step).wait()
        for k in range(COUPLED):
            for pair in range(32):
                rows_ref[pl.ds((k * 32 + pair) * STEP, STEP), :] = raw_ref[
                    step, k, :, pair * LANES : (pair + 1) * LANES
                ]
        for item in range(STEP):
            for duo in range(4):
                first = rows_ref[pl.ds(2 * duo * 256 + item, 32, stride=STEP), :]
                if 2 * duo + 1 < COUPLED:
                    second = rows_ref[pl.ds((2 * duo + 1) * 256 + item, 32, stride=STEP), :]
                else:
                    second = jnp.zeros_like(first)
                even = jnp.where(half, first, pltpu.roll(second, RHS, 1))
                odd = jnp.where(half, pltpu.roll(first, RHS, 1), second)
                if duo == 0:
                    even = even - shift_even
                    odd = odd - shift_odd
                lead, rest = halves_of(jnp.concatenate([even, odd], axis=0))
                block = step * STEP + item
                mats_ref[block, :BLOCK, duo * LANES : (duo + 1) * LANES] = lead
                mats_ref[block, BLOCK:, duo * LANES : (duo + 1) * LANES] = rest


def own_extended(parts_ref, extended_ref):
    extended_ref[:BLK_DEV] = parts_ref[...]


def fill_extended(odd, received, extended_ref):
    half = left_lanes(32)
    for side, got_ref in zip((1, 0, 3 - odd[0], 2 + odd[0]), received):
        for face in range(FACES):
            packed = got_ref[face * 32 : (face + 1) * 32, :]
            turned = pltpu.roll(packed, RHS, 1)
            block = BLK_DEV + side * FACES + face
            extended_ref[block, :32] = two_parts(jnp.where(half, packed, turned))
            extended_ref[block, 32:] = two_parts(jnp.where(half, turned, packed))


def block_row(block, neighbours, mats_ref, extended_ref, nodes_ref):
    pieces = [extended_ref[block]]
    for k in range(COUPLED - 1):
        pieces.append(extended_ref[neighbours[k, block]])
    pieces.append(pieces[0])
    grid = product(mats_ref[block], jnp.concatenate(pieces, axis=0))
    folded = grid[:BLOCK] + grid[BLOCK:]
    doubled = folded + pltpu.roll(folded, RHS, 1)
    start = block * BLOCK
    nodes_ref[pl.ds(start, 32, stride=2), :] = doubled[:32]
    nodes_ref[pl.ds(start + 1, 32, stride=2), :] = doubled[32:]
    return nodes_ref[pl.ds(start, BLOCK), :]


def first_kernel(
    neighbours_hbm, face_hbm, odd_hbm, mats_ref, parts_ref, own_ref, far, near, inner, outer,
    image_ref, both_ref, out0, out1, out2, out3, extended_ref, nodes_ref,
    neighbours, face_rows, odd, table_sems,
):
    waits = fetch_tables(
        (neighbours_hbm, face_hbm, odd_hbm), (neighbours, face_rows, odd), table_sems
    )
    own_extended(parts_ref, extended_ref)
    for wait in waits:
        wait.wait()
    fill_extended(odd, (far, near, inner, outer), extended_ref)
    for block in range(BLK_DEV):
        doubled = block_row(block, neighbours, mats_ref, extended_ref, nodes_ref)
        image_ref[block] = two_parts(doubled)
        rows = slice(block * BLOCK, (block + 1) * BLOCK)
        both_ref[rows, :] = jnp.where(left_lanes(BLOCK), own_ref[rows, :], doubled)
    emit_faces(face_rows, odd, nodes_ref, (out0, out1, out2, out3))


def quarter_sum(grid):
    tall = grid[:RHS] + grid[RHS:]
    return tall + pltpu.roll(tall, RHS, 1)


def rows_of(ref, step):
    return ref[step * STEP : (step + 1) * STEP].reshape(STEP * BLOCK, LANES)


def product(left, right):
    return jnp.dot(left, right, preferred_element_type=F32)


def gram_kernel(turned_ref, field_ref, image_ref, out_ref, image_turned_ref, wide_acc, acc_ref):
    wide_acc[...] = jnp.zeros_like(wide_acc)
    acc_ref[...] = jnp.zeros_like(acc_ref)
    for step in range(GRID):
        field = rows_of(field_ref, step)
        image = rows_of(image_ref, step)
        turned = image.T
        image_turned_ref[:, columns_of(step)] = turned
        wide_acc[...] += product(
            turned_ref[:, columns_of(step)], jnp.concatenate([field, image], axis=1)
        )
        acc_ref[...] += product(turned, image)
    out_ref[:RHS, :] = quarter_sum(wide_acc[:, :LANES])
    out_ref[RHS:LANES, :] = quarter_sum(wide_acc[:, LANES:])
    out_ref[LANES:, :] = quarter_sum(acc_ref[...])


def second_kernel(
    neighbours_hbm, odd_hbm, mats_ref, parts_ref, far, near, inner, outer, turned_ref, image_turned_ref,
    gram_ref, outgoing_ref, image_hbm, sums_ref, extended_ref, nodes_ref, image_ref, acc_ref, sem,
    neighbours, odd, table_sems,
):
    waits = fetch_tables((neighbours_hbm, odd_hbm), (neighbours, odd), table_sems)
    own_extended(parts_ref, extended_ref)
    for wait in waits:
        wait.wait()
    fill_extended(odd, (far, near, inner, outer), extended_ref)
    for block in range(BLK_DEV):
        doubled = block_row(block, neighbours, mats_ref, extended_ref, nodes_ref)
        image_ref[block] = two_parts(doubled)
    saving = pltpu.make_async_copy(image_ref, image_hbm, sem)
    saving.start()
    far_rows = image_ref[...].reshape(NODES_DEV, LANES)
    acc_ref[:LANES] = product(turned_ref[...], far_rows)
    acc_ref[LANES:] = product(image_turned_ref[...], far_rows)
    pack_sums(
        gram_ref[:RHS, :],
        gram_ref[RHS:LANES, :],
        gram_ref[LANES:, :],
        quarter_sum(acc_ref[:LANES]),
        quarter_sum(acc_ref[LANES:]),
        sums_ref,
    )
    saving.wait()


def pack_sums(norm, curve, image_norm, far_field, far_image, sums_ref):
    half = left_lanes(RHS)
    row = lax.broadcasted_iota(jnp.int32, (RHS, LANES), 0)
    col = lax.broadcasted_iota(jnp.int32, (RHS, LANES), 1)
    col = jnp.where(half, col, col - RHS)
    upper = row <= col
    diagonal = jnp.sum(jnp.where(row == col, image_norm, 0.0), axis=0, keepdims=True)
    last = jnp.where(row == RHS - 2, diagonal[:, RHS - 1 : RHS], diagonal)
    square = far_image[:, :RHS]
    balanced = 0.5 * (square + square.T)
    balanced = jnp.concatenate([balanced, balanced], axis=1)
    packed = jnp.where(upper, balanced, last)
    sums_ref[:RHS, :] = jnp.where(half, jnp.where(upper, norm, image_norm), curve)
    sums_ref[RHS:, :] = jnp.where(half, far_field, packed)


def unpack_sums(sums_ref):
    pair = sums_ref[:RHS, :RHS]
    curve = sums_ref[:RHS, RHS:]
    far_field = sums_ref[RHS:, :RHS]
    packed = sums_ref[RHS:, RHS:]
    row = lax.broadcasted_iota(jnp.int32, (RHS, RHS), 0)
    col = lax.broadcasted_iota(jnp.int32, (RHS, RHS), 1)
    pair_t = pair.T
    packed_t = packed.T
    norm = jnp.where(row <= col, pair, pair_t)
    lanes = lax.broadcasted_iota(jnp.int32, (1, RHS), 1)
    diagonal = jnp.where(
        lanes == RHS - 1, packed[RHS - 2 : RHS - 1, :1], packed[RHS - 1 : RHS, :]
    )
    image_norm = jnp.where(row > col, pair, pair_t)
    image_norm = jnp.where(row == col, diagonal, image_norm)
    far_image = jnp.where(row <= col, packed, packed_t)
    return norm, curve, image_norm, far_field, far_image


def relay_kernel(
    owners_hbm, node_hbm, both_ref, out_ref, counts, owners, die_node, table_sems
):
    waits = fetch_tables((owners_hbm, node_hbm), (owners, die_node), table_sems)
    out_ref[...] = jnp.zeros_like(out_ref)
    for owner in range(16):
        counts[owner] = owner * SLOTS
    for wait in waits:
        wait.wait()

    def move(row, carry):
        owner = owners[row]
        slot = counts[owner]
        counts[owner] = slot + 1
        out_ref[pl.ds(slot, 1), :] = both_ref[pl.ds(die_node[row], 1), :]
        return carry

    lax.fori_loop(0, DIE_ROWS, move, 0, unroll=8)


def mul(left, right):
    return jnp.dot(left, right, precision=lax.Precision.HIGHEST, preferred_element_type=F32)


def mul_t(left, right):
    return lax.dot_general(
        left,
        right,
        (((1,), (1,)), ((), ())),
        precision=lax.Precision.HIGHEST,
        preferred_element_type=F32,
    )


def eliminate(systems):
    tall = 8
    spread = (tall, LANES)
    sub = lax.broadcasted_iota(jnp.int32, spread, 0)
    grids = [[system[tall * r : tall * r + tall] for r in range(RHS // tall)] for system in systems]
    for pivot in range(RHS // tall):
        base = tall * pivot
        for tiles in grids:
            rows = tiles[pivot]
            entry = {
                (i, j): jnp.broadcast_to(rows[i : i + 1, base + j : base + j + 1], spread)
                for i in range(tall)
                for j in range(i + 1)
            }
            inverse, lower = [], {}
            for r in range(tall):
                inverse.append(1.0 / entry[r, r])
                for i in range(r + 1, tall):
                    lower[i, r] = entry[i, r] * inverse[r]
                    for j in range(r + 1, i + 1):
                        entry[i, j] = entry[i, j] - lower[i, r] * entry[j, r]
            solved = [jnp.broadcast_to(rows[i : i + 1, :], spread) for i in range(tall)]
            for i in range(tall):
                for j in range(i):
                    solved[i] = solved[i] - lower[i, j] * solved[j]
            for i in reversed(range(tall)):
                solved[i] = solved[i] * inverse[i]
                for j in range(i + 1, tall):
                    solved[i] = solved[i] - lower[j, i] * solved[j]
            for r in range(RHS // tall):
                if r == pivot:
                    continue
                old = tiles[r]
                fresh = old
                for i in range(tall):
                    fresh = fresh - old[:, base + i : base + i + 1] * solved[i]
                tiles[r] = fresh
            merged = solved[0]
            for i in range(1, tall):
                merged = jnp.where(sub == i, solved[i], merged)
            tiles[pivot] = merged
    return [jnp.concatenate(tiles, axis=0)[:, RHS:] for tiles in grids]


def wide(left, right):
    return jnp.concatenate([left, right], axis=1)


def solve_steps(sums_ref):
    norm_zero, cross, image_norm, far_field, far_image = unpack_sums(sums_ref)
    eye = (
        lax.broadcasted_iota(jnp.int32, (RHS, RHS), 0)
        == lax.broadcasted_iota(jnp.int32, (RHS, RHS), 1)
    ).astype(F32)
    curve_zero = 0.5 * (cross + cross.T) + SHIFT * norm_zero
    alpha, norm_inverse = eliminate([wide(curve_zero, norm_zero), wide(norm_zero, eye)])
    alpha_t = alpha.T
    gram = jnp.concatenate([wide(norm_zero, cross), wide(cross.T, image_norm)], axis=0)
    shifted = jnp.concatenate([wide(cross, far_field), wide(image_norm, far_image)], axis=0)
    start = eye - SHIFT * alpha_t
    resid = wide(start, -alpha_t)
    norm_one = mul_t(mul(resid, gram), resid)
    mixed = start + mul(norm_inverse, norm_one).T
    direction = wide(mixed, -alpha_t)
    curve_one = mul_t(mul(direction, shifted + SHIFT * gram), direction)
    (alpha_two,) = eliminate([wide(0.5 * (curve_one + curve_one.T), norm_one)])
    second = mul(alpha_two.T, wide(mixed, alpha_t))
    gain, drop = second[:, :RHS], second[:, RHS:]
    keep = alpha_t + gain
    return keep, drop, start - SHIFT * gain, keep - SHIFT * drop


def halves_of(value):
    lead = value.astype(BF16)
    return lead, (value - lead.astype(F32)).astype(BF16)


def final_kernel(
    sums_ref, turned_ref, image_turned_ref, far_hbm, solution_hbm, residual_hbm, coef_ref,
    far_ref, solution_ref, residual_ref, far_sem, sems,
):
    fetch = pltpu.make_async_copy(far_hbm, far_ref, far_sem)
    fetch.start()
    keep, drop, left_over, taken = solve_steps(sums_ref)
    top = [wide(keep, keep), wide(-drop, -drop), jnp.zeros((RHS, LANES), F32)]
    low = [wide(left_over, left_over), wide(-taken, -taken), wide(drop, drop)]
    rows = jnp.concatenate(
        [jnp.concatenate(top, axis=1), jnp.concatenate(low, axis=1)], axis=0
    )
    weights = jnp.concatenate(halves_of(rows), axis=0)
    coef_ref[...] = jnp.concatenate([keep.T, -drop.T], axis=0)
    fetch.wait()
    copies = []
    for step in range(GRID):
        columns = columns_of(step)
        both = jnp.concatenate([turned_ref[:, columns], image_turned_ref[:, columns]], axis=0)
        mixed = product(weights[:, : 2 * LANES], both) + lax.dot_general(
            weights[:, 2 * LANES :],
            rows_of(far_ref, step),
            (((1,), (1,)), ((), ())),
            preferred_element_type=F32,
        )
        mixed = mixed[:LANES] + mixed[LANES:]
        solution_ref[:, columns] = mixed[:RHS]
        residual_ref[:, columns] = mixed[RHS:]
        part = pl.ds(step * STEP * BLOCK, STEP * BLOCK)
        for at, (source, target) in enumerate(
            ((solution_ref, solution_hbm), (residual_ref, residual_hbm))
        ):
            copies.append(
                pltpu.make_async_copy(source.at[:, part], target.at[:, part], sems.at[at, step])
            )
            copies[-1].start()
    for copy in copies:
        copy.wait()


def owner_kernel(coef_ref, got_ref, out_hbm, out_ref, sems):
    coef = coef_ref[...]
    none = jnp.zeros_like(coef)
    square = jnp.concatenate([wide(coef, none), wide(none, coef)], axis=0)
    weights = jnp.concatenate(halves_of(square), axis=1)

    def save(at):
        part = pl.ds(at * 32 * LANES, 32 * LANES)
        return pltpu.make_async_copy(out_ref.at[:, part], out_hbm.at[:, part], sems.at[at])

    for pack in range(8):
        pieces = []
        for pair in range(8 * pack, 8 * pack + 8):
            pieces.append(
                wide(
                    got_ref[pl.ds(2 * pair, 16, stride=SLOTS), :],
                    got_ref[pl.ds(2 * pair + 1, 16, stride=SLOTS), :],
                )
            )
        rows = jnp.concatenate(pieces, axis=0)
        lead, rest = halves_of(rows)
        grid = product(jnp.concatenate([lead, rest], axis=0), weights)
        grid = grid[:LANES] + grid[LANES:]
        grid = grid[:, :LANES] + grid[:, LANES:]
        for at in range(8):
            pair = 8 * pack + at
            out_ref[:, pair * LANES : (pair + 1) * LANES] = grid[16 * at : 16 * at + 16]
        if pack % 4 == 3:
            save(pack // 4).start()
    for at in range(2):
        save(at).wait()


def swap(shard, axis, bit):
    return lax.ppermute(shard, axis, [(i, i ^ bit) for i in range(lax.axis_size(axis))])


def exchange(faces):
    count = lax.axis_size("layer")
    top = lax.axis_size("region") // 2
    far = swap(faces[0], "region", top)
    near = swap(faces[1], "region", 1)
    inner = swap(faces[2], "layer", 1)
    pairs = [(i, i + 1) for i in range(1, count - 1, 2)]
    outer = lax.ppermute(faces[3], "layer", pairs + [(b, a) for a, b in pairs])
    return far, near, inner, outer


def total(local):
    layers = lax.axis_size("layer")
    regions = lax.axis_size("region")
    parts = local.reshape(layers, LANES // layers, LANES)
    mine = jnp.sum(lax.all_to_all(parts, "layer", 0, 0, tiled=True), axis=0)
    copies = jnp.broadcast_to(mine[None], (regions,) + mine.shape)
    mine = jnp.sum(lax.all_to_all(copies, "region", 0, 0, tiled=True), axis=0)
    copies = jnp.broadcast_to(mine[None], (layers,) + mine.shape)
    return lax.all_to_all(copies, "layer", 0, 0, tiled=True).reshape(LANES, LANES)


TURNED = jax.ShapeDtypeStruct((LANES, NODES_DEV), BF16)
PARTS = jax.ShapeDtypeStruct((BLK_DEV, BLOCK, LANES), BF16)
NODE_ROWS = jax.ShapeDtypeStruct((NODES_DEV, LANES), F32)
FACE = jax.ShapeDtypeStruct((FACES * 32, LANES), F32)
FIELD = jax.ShapeDtypeStruct((RHS, NODES_DEV), F32)


def on_device(right_side, block_entries, neighbours, face_rows, die_owner, die_node):
    owners = in_hbm(die_owner[:, 0])
    die_node = in_hbm(die_node)
    neighbours = in_hbm(neighbours.T)
    face_rows = in_hbm(face_rows)
    odd = (lax.axis_index("layer") % 2).astype(jnp.int32).reshape(1)
    entries = in_hbm(jnp.transpose(block_entries, (1, 0, 2)))
    right_side = in_hbm(right_side)
    outcome = pl.pallas_call(
        field_kernel,
        in_specs=[pl.BlockSpec(memory_space=pl.ANY)] * 3,
        out_specs=[resident()] * 6,
        out_shape=[FIELD, NODE_ROWS] + [FACE] * 4,
        scratch_shapes=[pltpu.SemaphoreType.DMA((GRID,))] + tables((4, FACES), (1,)),
        compiler_params=params(8),
        cost_estimate=cost(1_000_000, 5_000_000),
        name="field",
    )(face_rows, odd, right_side)
    right_rows, own_rows, faces = outcome[0], outcome[1], outcome[2:]
    received = exchange(faces)
    mats, field, turned = pl.pallas_call(
        entries_kernel,
        in_specs=[pl.BlockSpec(memory_space=pl.ANY)] + [resident()] * 2,
        out_specs=[resident()] * 3,
        out_shape=[
            jax.ShapeDtypeStruct((BLK_DEV, 2 * BLOCK, 4 * LANES), BF16),
            PARTS,
            TURNED,
        ],
        scratch_shapes=[
            pltpu.VMEM((GRID, COUPLED, STEP, BLOCK * BLOCK), F32),
            pltpu.VMEM((COUPLED * 32 * STEP, LANES), F32),
            pltpu.SemaphoreType.DMA((GRID,)),
        ],
        compiler_params=params(12),
        cost_estimate=cost(10_000_000, 16_000_000),
        name="entries",
    )(entries, right_rows, own_rows)
    apply_scratch = [
        pltpu.VMEM((BLK_DEV + 4 * FACES, BLOCK, LANES), BF16),
        pltpu.VMEM((NODES_DEV, LANES), F32),
    ]
    outcome = pl.pallas_call(
        first_kernel,
        in_specs=[pl.BlockSpec(memory_space=pl.ANY)] * 3 + [resident()] * 7,
        out_specs=[resident()] * 6,
        out_shape=[PARTS, NODE_ROWS] + [FACE] * 4,
        scratch_shapes=apply_scratch + tables((COUPLED - 1, BLK_DEV), (4, FACES), (1,)),
        compiler_params=params(8),
        cost_estimate=cost(1_000_000_000, 16_000_000),
        name="first_image",
    )(neighbours, face_rows, odd, mats, field, own_rows, *received)
    image, both_rows, faces = outcome[0], outcome[1], outcome[2:]
    received = exchange(faces)
    grams, image_turned = pl.pallas_call(
        gram_kernel,
        in_specs=[resident()] * 3,
        out_specs=[resident()] * 2,
        out_shape=[jax.ShapeDtypeStruct((3 * RHS, LANES), F32), TURNED],
        scratch_shapes=[pltpu.VMEM((LANES, 2 * LANES), F32), pltpu.VMEM((LANES, LANES), F32)],
        compiler_params=params(8),
        cost_estimate=cost(500_000_000, 2_000_000),
        name="near_grams",
    )(turned, field, image)
    outgoing = pl.pallas_call(
        relay_kernel,
        in_specs=[pl.BlockSpec(memory_space=pl.ANY)] * 2 + [resident()],
        out_specs=resident(),
        out_shape=jax.ShapeDtypeStruct((16 * SLOTS, LANES), F32),
        scratch_shapes=[pltpu.SMEM((16,), jnp.int32)] + tables((DIE_ROWS,), (DIE_ROWS,)),
        compiler_params=params(8),
        cost_estimate=cost(1_000_000, 10_000_000),
        name="relay_rows",
    )(owners, die_node, both_rows)
    relayed = lax.all_to_all(
        outgoing.reshape(16, SLOTS, LANES), "layer", 0, 0, tiled=True
    ).reshape(16 * SLOTS, LANES)
    far_image, local_sums = pl.pallas_call(
        second_kernel,
        in_specs=[pl.BlockSpec(memory_space=pl.ANY)] * 2
        + [resident()] * 9
        + [pl.BlockSpec(memory_space=pl.ANY)],
        out_specs=[far_memory(), resident()],
        out_shape=[
            pltpu.HBM(PARTS.shape, BF16),
            jax.ShapeDtypeStruct((LANES, LANES), F32),
        ],
        scratch_shapes=apply_scratch
        + [
            pltpu.VMEM(PARTS.shape, BF16),
            pltpu.VMEM((2 * LANES, LANES), F32),
            pltpu.SemaphoreType.DMA,
        ]
        + tables((COUPLED - 1, BLK_DEV), (1,)),
        compiler_params=params(8),
        cost_estimate=cost(1_000_000_000, 14_000_000),
        name="second_image",
    )(neighbours, odd, mats, image, *received, turned, image_turned, grams, outgoing)
    sums = total(local_sums)
    solution_field, residual, coef = pl.pallas_call(
        final_kernel,
        in_specs=[resident()] * 3 + [far_memory()],
        out_specs=[far_memory()] * 2 + [resident()],
        out_shape=[FIELD, FIELD, jax.ShapeDtypeStruct((LANES, RHS), F32)],
        scratch_shapes=[
            pltpu.VMEM(PARTS.shape, BF16),
            pltpu.VMEM(FIELD.shape, F32),
            pltpu.VMEM(FIELD.shape, F32),
            pltpu.SemaphoreType.DMA,
            pltpu.SemaphoreType.DMA((2, GRID)),
        ],
        compiler_params=params(8),
        cost_estimate=cost(500_000_000, 8_000_000),
        name="final",
    )(sums, turned, image_turned, in_hbm(far_image))
    mech_temps = pl.pallas_call(
        owner_kernel,
        in_specs=[resident()] * 2,
        out_specs=far_memory(),
        out_shape=jax.ShapeDtypeStruct((16, SLOTS * RHS), F32),
        scratch_shapes=[
            pltpu.VMEM((16, SLOTS * RHS), F32),
            pltpu.SemaphoreType.DMA((2,)),
        ],
        compiler_params=params(8),
        cost_estimate=cost(100_000_000, 2_000_000),
        name="owner_rows",
    )(coef, relayed)
    return solution_field, residual, mech_temps


def solution(mesh):
    in_specs = (
        P(None, ("region", "layer")),
        P(("region", "layer"), None, None),
        P(("region", "layer"), None),
        P(("region", "layer"), None),
        P(("region", "layer"), None),
        P(("region", "layer")),
    )
    out_specs = (
        P(None, ("region", "layer")),
        P(None, ("region", "layer")),
        P(("region", "layer"), None),
    )
    return jax.shard_map(
        on_device, mesh=mesh, in_specs=in_specs, out_specs=out_specs, check_vma=False
    )
```
